32 devices in a mesh: region: 2 (over y), tile: 4 (over z), member: 2 (over x), date: 2 (over core).
Axes of the slice: x: 2, y: 2, z: 4, core: 2. Of those that a mesh axis runs over, the one named last changes fastest.
Arguments:
- sim_lai: bfloat16 [2, 32, 4, 32, 512], P('date', ('region', 'tile'), 'member'), parts along dimension 1, may hold values from 0 to 6
- owner_ids: int32 [2, 32], P('date', ('region', 'tile')), parts along dimension 1, may hold values from 0 to 3, as said below
- cloud_words: int32 [2, 32, 32], P('date', ('region', 'tile')), parts along dimension 1, may hold values from -2147483648 to 2147483646
- scene_lai: bfloat16 [2, 8, 8, 16, 256], P('date', ('region', 'tile'), 'member'), parts along dimension 1, may hold values from 0 to 6
- scene_sigma: bfloat16 [2, 8, 8, 16, 256], P('date', ('region', 'tile'), 'member'), parts along dimension 1, may hold values from 1 to 4
- mtf_taps: float32 [2, 7], replicated, may hold values from 0.1 to 1
Outputs:
- lai_update: bfloat16 [2, 32, 4, 32, 512], P('date', ('region', 'tile'), 'member'), parts along dimension 1
The draws below stay inside these ranges and needn't reach their ends.
There are 2 independent parts, one for each index of `region`. The reference program is written for one: setup_inputs(seed, part) draws one part's arguments, and reference() takes and returns one part's arrays. A program takes and returns all parts, laid end to end along the dimension named above; an argument that names none is the same for every part. Nothing has to cross between parts.
Inputs may be any that keep to these rules, and one draw needn't show every extreme that they name: `owner_ids`: on each date each device along tile, holding 4 consecutive tiles, sends either none or exactly 2 of them to each owner; some owner receives 2 tiles from every device.
All inputs are finite; a program needn't handle non-finite values.
Results may differ from the reference program's by a relative error of at most 0.013.
The reference program's roundings to bfloat16 on the way (of `row_table`, `col_table`, `blurred`, `predicted`, `misfit` and `spread`) count: a program that leaves them out, or rounds other values in their place, can miss the bound.
Values may be sent and summed in bfloat16 or wider, within the bound.
No kernel may reach another device: no remote copies, remote signals or barrier semaphores. Data moves between devices by JAX's collectives and lax.ppermute only.
A program may use at most 64 MiB of HBM per device.

```python
import math
import jax
import jax.numpy as jnp
from jax import lax

COLS = 512
ROWS = 32
CAP = 2
TAPS = 7
PICKS = 2
NHOT = 1
TILES_DEV = 4
TILES = 16
MEMBERS = 4
DATES = 2
SLOTS = 8
HALF_R = 16
HALF_C = 256
MASK_WORDS = 32
N_TILE = 4


def draw_owner_ids(key, part):

    def one_date(date_key):
        key_order, key_offset, key_shuffle = jax.random.split(date_key, 3)
        order = jax.random.permutation(key_order, N_TILE).astype(jnp.int32)
        hot_owners = order[:NHOT]
        cold_owners = order[NHOT:]
        offsets = jax.random.randint(key_offset, (N_TILE,), 0, N_TILE - NHOT)
        cold_index = (offsets[:, None] + jnp.arange(PICKS - NHOT)[None, :]) % (N_TILE - NHOT)
        cold_picks = cold_owners[cold_index]
        all_picks = jnp.concatenate([jnp.broadcast_to(hot_owners[None, :], (N_TILE, NHOT)), cold_picks], axis=1)
        repeated = jnp.repeat(all_picks, CAP, axis=1)
        shuffle_keys = jax.random.split(key_shuffle, N_TILE)
        orders = jax.vmap(lambda single: jax.random.permutation(single, TILES_DEV))(shuffle_keys)
        shuffled = jnp.take_along_axis(repeated, orders, axis=1)
        return shuffled.reshape(-1)
    date_keys = jax.random.split(jax.random.fold_in(key, 17), DATES)
    return jax.vmap(one_date)(date_keys).astype(jnp.int32)


def plant(drawn, own_key, low, top_value):
    place = [jax.random.randint(jax.random.fold_in(own_key, axis), (), 0, length) for axis, length in enumerate(drawn.shape)]
    main_axis = drawn.shape.index(max(drawn.shape))
    next_to = place[:main_axis] + [(place[main_axis] + 1) % drawn.shape[main_axis]] + place[main_axis + 1:]
    return drawn.at[tuple(place)].set(low).at[tuple(next_to)].set(top_value)


def levels(key, extent, cuts, least, high):
    gain = 1.0
    for dim, blocks in cuts:
        steps = jax.random.uniform(jax.random.fold_in(jax.random.fold_in(key, 6), dim), (blocks,), jnp.float32, least / len(cuts), high / len(cuts))
        gain = gain * jnp.repeat(jnp.exp(steps), extent[dim] // blocks).reshape((-1,) + (1,) * (len(extent) - 1 - dim))
    return gain


def setup_inputs(seed: int = 0, part: int = 0) -> dict:
    splits = jax.random.split(jax.random.key(seed), 7)
    part_splits = jax.random.split(jax.random.fold_in(splits[6], part), 7)
    return {
        "sim_lai": jnp.clip(6.0 * jax.random.uniform(part_splits[0], (DATES, TILES, MEMBERS, ROWS, COLS), jnp.float32) ** levels(part_splits[0], (DATES, TILES, MEMBERS, ROWS, COLS), ((0, 2), (1, 4), (2, 2)), -0.2, 0.2), 0.0, 6.0).astype(jnp.bfloat16),
        "owner_ids": draw_owner_ids(jax.random.fold_in(jax.random.fold_in(splits[6], part), 71), part),
        "cloud_words": plant(jax.random.randint(part_splits[2], (DATES, TILES, MASK_WORDS), -2147483648, 2147483647), jax.random.fold_in(part_splits[2], 1), -2147483648, 2147483646).astype(jnp.int32),
        "scene_lai": jnp.clip(6.0 * jax.random.uniform(part_splits[3], (DATES, N_TILE, SLOTS, HALF_R, HALF_C), jnp.float32) ** levels(part_splits[3], (DATES, N_TILE, SLOTS, HALF_R, HALF_C), ((0, 2), (1, 4), (2, 2)), -0.2, 0.2), 0.0, 6.0).astype(jnp.bfloat16),
        "scene_sigma": jnp.clip(jnp.exp(math.log(4.0) - 1.3862944 * jax.random.uniform(part_splits[4], (DATES, N_TILE, SLOTS, HALF_R, HALF_C), jnp.float32) ** levels(part_splits[4], (DATES, N_TILE, SLOTS, HALF_R, HALF_C), ((0, 2), (1, 4), (2, 2)), -0.2, 0.2)), 1.0, 4.0).astype(jnp.bfloat16),
        "mtf_taps": jnp.clip(jnp.exp(jax.random.uniform(splits[5], (2, TAPS), jnp.float32, math.log(0.1), math.log(1.0))), 0.1, 1.0),
    }


def band_tables(mtf_taps, tile_rows, tile_cols):
    kernel = mtf_taps / jnp.sum(mtf_taps, axis=1, keepdims=True)
    half_rows = tile_rows // 2
    half_cols = tile_cols // 2
    tap_reach = mtf_taps.shape[1] // 2
    out_rows = lax.broadcasted_iota(jnp.int32, (half_rows, tile_rows), 0)
    in_rows = lax.broadcasted_iota(jnp.int32, (half_rows, tile_rows), 1)
    in_cols = lax.broadcasted_iota(jnp.int32, (tile_cols, half_cols), 0)
    out_cols = lax.broadcasted_iota(jnp.int32, (tile_cols, half_cols), 1)
    row_table = jnp.zeros((half_rows, tile_rows), jnp.float32)
    col_table = jnp.zeros((tile_cols, half_cols), jnp.float32)
    for offset in range(mtf_taps.shape[1]):
        row_table = row_table + jnp.where(in_rows == 2 * out_rows + offset - tap_reach, kernel[0, offset], 0.0)
        col_table = col_table + jnp.where(in_cols == 2 * out_cols + offset - tap_reach, kernel[1, offset], 0.0)
    return row_table.astype(jnp.bfloat16), col_table.astype(jnp.bfloat16)


def cloud_weights(words, half_rows, half_cols):
    shifts = jnp.arange(32).astype(jnp.int32)
    bit_values = jnp.bitwise_and(jnp.right_shift(words[..., None], shifts), 1)
    cells = bit_values.reshape(words.shape[:-1] + (half_rows // 2, half_cols // 2)).astype(jnp.float32)
    return jnp.repeat(jnp.repeat(cells, 2, axis=-2), 2, axis=-1)


def weighted_misfit(valid, observed, sigma_obs, predicted):
    sigma_wide = sigma_obs.astype(jnp.float32)
    gap = observed.astype(jnp.float32) - predicted.astype(jnp.float32)
    return (valid * gap / (sigma_wide * sigma_wide)).astype(jnp.bfloat16)


def degrade_ref(fields, row_table, col_table):
    blurred = jnp.einsum('ir,...rc->...ic', row_table.astype(jnp.float32), fields.astype(jnp.float32)).astype(jnp.bfloat16)
    return jnp.einsum('...ic,cj->...ij', blurred.astype(jnp.float32), col_table.astype(jnp.float32)).astype(jnp.bfloat16)


def adjoint_ref(misfit, row_table, col_table):
    spread = jnp.einsum('...ij,cj->...ic', misfit.astype(jnp.float32), col_table.astype(jnp.float32)).astype(jnp.bfloat16)
    return jnp.einsum('ir,...ic->...rc', row_table.astype(jnp.float32), spread.astype(jnp.float32)).astype(jnp.bfloat16)


def reference(sim_lai, owner_ids, cloud_words, scene_lai, scene_sigma, mtf_taps):
    row_table, col_table = band_tables(mtf_taps, ROWS, COLS)
    grouped = owner_ids.reshape(DATES, N_TILE, TILES_DEV)
    same_owner = grouped[..., :, None] == grouped[..., None, :]
    earlier = lax.broadcasted_iota(jnp.int32, (TILES_DEV, TILES_DEV), 0) < lax.broadcasted_iota(jnp.int32, (TILES_DEV, TILES_DEV), 1)
    rank = jnp.sum(jnp.logical_and(same_owner, earlier).astype(jnp.int32), axis=-2).reshape(DATES, TILES)
    source = (jnp.arange(TILES) // TILES_DEV).astype(jnp.int32)
    slot = (source[None, :] * CAP + rank).astype(jnp.int32)
    date_index = jnp.arange(DATES).astype(jnp.int32)[:, None]
    observed = scene_lai[date_index, owner_ids, slot]
    sigma_obs = scene_sigma[date_index, owner_ids, slot]
    valid = cloud_weights(cloud_words, HALF_R, HALF_C)

    def per_date(inputs):
        fields, seen, sigma_here, valid_here = inputs
        predicted = degrade_ref(fields, row_table, col_table)
        misfit = weighted_misfit(valid_here[:, None], seen[:, None], sigma_here[:, None], predicted)
        return adjoint_ref(misfit, row_table, col_table)

    return lax.map(per_date, (sim_lai, observed, sigma_obs, valid))
```

```python
import math

import jax
import jax.numpy as jnp
import numpy as np
from jax import lax
from jax.experimental import pallas as pl
from jax.experimental.pallas import tpu as pltpu
from jax.sharding import PartitionSpec as P

CAP = 2
GROUP = ("tile", "member")


def plan(n_tile, n_mem):
    per = n_tile // n_mem
    steps = []
    table = np.zeros((n_tile * n_mem, n_tile), np.int32)
    for k in range(per):
        for j in range(n_mem):
            pairs, block = [], np.zeros((n_tile * n_mem,), np.int32)
            for o in range(n_tile):
                for mm in range(n_mem):
                    a = (o % per + k) % per
                    m = (o // per + j) % n_mem
                    s = mm * per + a
                    pairs.append((o * n_mem + mm, s * n_mem + m))
                    block[o * n_mem + mm] = a
                    table[s * n_mem + m, o] = len(steps)
            steps.append((pairs, block))
    return steps, table


def chunk_tiles(tiles, members, rows):
    best = 1
    for c in range(1, tiles + 1):
        if tiles % c == 0 and c * members * rows <= 256:
            best = c
    return best


def iota(shape, dim):
    return lax.broadcasted_iota(jnp.int32, shape, dim)


def pick(which, taps, row):
    out = jnp.zeros(which.shape, jnp.float32)
    for k in range(taps.shape[1]):
        out = jnp.where(which == k, taps[row : row + 1, k : k + 1], out)
    return out.astype(jnp.bfloat16)


def before(sizes, taps_ref, words_ref, field_ref, pred_ref, valid_ref, colt_ref, rowt_ref, pad):
    tiles, chunk, members, rows, cols = sizes
    half_r, half_c = rows // 2, cols // 2
    n_words = words_ref.shape[1]
    taps = taps_ref[...]
    taps = taps / jnp.sum(taps, axis=1, keepdims=True)
    reach = taps.shape[1] // 2
    fields = chunk * members
    fr, fh = fields * rows, fields * half_r
    i, r = iota((fh, fr), 0), iota((fh, fr), 1)
    row_bd = jnp.where(
        i // half_r == r // rows, r % rows - 2 * (i % half_r) + reach, -1
    )
    row_bd = pick(row_bd, taps, 0)
    i, r = iota((fr, fh), 1), iota((fr, fh), 0)
    rowt = jnp.where(i // half_r == r // rows, r % rows - 2 * (i % half_r) + reach, -1)
    rowt_ref[...] = pick(rowt, taps, 0)
    col = pick(iota((cols, half_c), 0) - 2 * iota((cols, half_c), 1) + reach, taps, 1)
    colt_ref[...] = pick(iota((half_c, cols), 1) - 2 * iota((half_c, cols), 0) + reach, taps, 1)
    for g in range(tiles // chunk):
        field = field_ref[g * fr : (g + 1) * fr, :]
        blurred = jnp.dot(row_bd, field, preferred_element_type=jnp.float32).astype(jnp.bfloat16)
        pred_ref[g * fh : (g + 1) * fh, :] = jnp.dot(
            blurred, col, preferred_element_type=jnp.float32
        ).astype(jnp.bfloat16)
    pad[...] = jnp.zeros(pad.shape, jnp.int32)
    pad[:, :n_words] = words_ref[...]
    per_row = half_c // 2 // 32
    for t in range(tiles):
        words = jnp.broadcast_to(pad[t : t + 1, :], (8, 128))
        for i0 in range(0, half_r, 8):
            for j0 in range(0, half_c, 128):
                i = iota((8, 128), 0) + i0
                j = iota((8, 128), 1) + j0
                word = jnp.take_along_axis(words, i // 2 * per_row + j // 64, axis=1)
                bit = jnp.bitwise_and(jnp.right_shift(word, j // 2 % 32), 1)
                valid_ref[t * half_r + i0 : t * half_r + i0 + 8, j0 : j0 + 128] = bit.astype(jnp.float32)


def after(sizes, n_steps, owners_ref, table_ref, pred_ref, valid_ref, colt_ref, rowt_ref, *refs):
    tiles, chunk, members, rows, cols = sizes
    half_r, half_c = rows // 2, cols // 2
    arrived, out_ref, scenes = refs[:n_steps], refs[n_steps], refs[n_steps + 1]
    fields = chunk * members
    fr, fh = fields * rows, fields * half_r
    device = lax.axis_index(GROUP)
    for p in range(n_steps):
        scenes[p] = arrived[p][...]
    owner = [owners_ref[0, t] for t in range(tiles)]
    for g in range(tiles // chunk):
        parts = []
        for t in range(g * chunk, (g + 1) * chunk):
            rank = 0
            for u in range(t):
                rank = rank + jnp.where(owner[u] == owner[t], 1, 0)
            step = table_ref[device, owner[t]]
            seen = scenes[step, 0, rank].astype(jnp.float32)
            sigma = scenes[step, 1, rank].astype(jnp.float32)
            weight = valid_ref[t * half_r : (t + 1) * half_r, :] / (sigma * sigma)
            for m in range(members):
                at = (t * members + m) * half_r
                gap = seen - pred_ref[at : at + half_r, :].astype(jnp.float32)
                parts.append((gap * weight).astype(jnp.bfloat16))
        misfit = jnp.concatenate(parts, axis=0)
        spread = jnp.dot(misfit, colt_ref[...], preferred_element_type=jnp.float32).astype(jnp.bfloat16)
        out_ref[g * fr : (g + 1) * fr, :] = jnp.dot(
            rowt_ref[...], spread, preferred_element_type=jnp.float32
        ).astype(jnp.bfloat16)


def per_device(sim_lai, owner_ids, cloud_words, scene_lai, scene_sigma, mtf_taps):
    n_tile, n_mem = lax.axis_size("tile"), lax.axis_size("member")
    _, tiles, members, rows, cols = sim_lai.shape
    half_r, half_c = rows // 2, cols // 2
    steps, table = plan(n_tile, n_mem)
    per = n_tile // n_mem
    both = jnp.stack([scene_lai[0, 0], scene_sigma[0, 0]], 0)
    device = lax.axis_index(GROUP)
    blocks = {}
    arrived = []
    for pairs, block in steps:
        key = tuple(block)
        if key not in blocks:
            a = jnp.asarray(block)[device]
            blocks[key] = lax.dynamic_slice_in_dim(both, a * CAP, CAP, 1)
        arrived.append(lax.ppermute(blocks[key], GROUP, pairs))
    chunk = chunk_tiles(tiles, members, rows)
    sizes = (tiles, chunk, members, rows, cols)
    fields = chunk * members
    fr, fh = fields * rows, fields * half_r
    vmem = pl.BlockSpec(memory_space=pltpu.VMEM)
    smem = pl.BlockSpec(memory_space=pltpu.SMEM)
    pred, valid, colt, rowt = pl.pallas_call(
        lambda *refs: before(sizes, *refs),
        out_shape=(
            jax.ShapeDtypeStruct((tiles * members * half_r, half_c), jnp.bfloat16),
            jax.ShapeDtypeStruct((tiles * half_r, half_c), jnp.float32),
            jax.ShapeDtypeStruct((half_c, cols), jnp.bfloat16),
            jax.ShapeDtypeStruct((fr, fh), jnp.bfloat16),
        ),
        in_specs=[vmem] * 3,
        out_specs=[vmem] * 4,
        scratch_shapes=[pltpu.VMEM((tiles, 128), jnp.int32)],
        name="before",
    )(mtf_taps, cloud_words[0], sim_lai.reshape(tiles * members * rows, cols))
    out = pl.pallas_call(
        lambda *refs: after(sizes, len(steps), *refs),
        out_shape=jax.ShapeDtypeStruct((tiles * members * rows, cols), jnp.bfloat16),
        in_specs=[smem, smem] + [vmem] * (4 + len(steps)),
        out_specs=vmem,
        scratch_shapes=[pltpu.VMEM((len(steps), 2, CAP, half_r, half_c), jnp.bfloat16)],
        name="after",
    )(owner_ids, jnp.asarray(table), pred, valid, colt, rowt, *arrived)
    return out.reshape(sim_lai.shape)


def solution(mesh):
    placed = (
        P("date", ("region", "tile"), "member", None, None),
        P("date", ("region", "tile")),
        P("date", ("region", "tile"), None),
        P("date", ("region", "tile"), "member", None, None),
        P("date", ("region", "tile"), "member", None, None),
        P(),
    )
    return jax.shard_map(
        per_device,
        mesh=mesh,
        in_specs=placed,
        out_specs=P("date", ("region", "tile"), "member", None, None),
        check_vma=False,
    )
```

```python
import jax
import jax.numpy as jnp
from jax import lax
from jax.experimental import pallas as pl
from jax.experimental.pallas import tpu as pltpu
from jax.sharding import PartitionSpec as P

CAP = 2
GROUP = ("tile", "member")


def plan(n_tile, n_mem):
    per = n_tile // n_mem
    steps = []
    for k in range(per):
        for j in range(n_mem):
            pairs = []
            for o in range(n_tile):
                for mm in range(n_mem):
                    s = mm * per + (o + k) % per
                    m = (o // per + j) % n_mem
                    if (s, m) != (o, mm):
                        pairs.append((o * n_mem + mm, s * n_mem + m))
            steps.append((k, j, pairs))
    return steps


def chunk_tiles(tiles, members, rows):
    best = 1
    for c in range(1, tiles + 1):
        if tiles % c == 0 and c * members * rows <= 256:
            best = c
    return best


def iota(shape, dim):
    return lax.broadcasted_iota(jnp.int32, shape, dim)


def pick(which, taps, row):
    out = jnp.zeros(which.shape, jnp.float32)
    for k in range(taps.shape[1]):
        out = jnp.where(which == k, taps[row : row + 1, k : k + 1], out)
    return out.astype(jnp.bfloat16)


def before(sizes, taps_ref, words_ref, field_ref, pred_ref, valid_ref, colt_ref, rowt_ref, pad):
    tiles, chunk, members, rows, cols = sizes
    half_r, half_c = rows // 2, cols // 2
    n_words = words_ref.shape[1]
    taps = taps_ref[...]
    taps = taps / jnp.sum(taps, axis=1, keepdims=True)
    reach = taps.shape[1] // 2
    fields = chunk * members
    fr, fh = fields * rows, fields * half_r
    i, r = iota((fh, fr), 0), iota((fh, fr), 1)
    row_bd = jnp.where(
        i // half_r == r // rows, r % rows - 2 * (i % half_r) + reach, -1
    )
    row_bd = pick(row_bd, taps, 0)
    i, r = iota((fr, fh), 1), iota((fr, fh), 0)
    rowt = jnp.where(i // half_r == r // rows, r % rows - 2 * (i % half_r) + reach, -1)
    rowt_ref[...] = pick(rowt, taps, 0)
    col = pick(iota((cols, half_c), 0) - 2 * iota((cols, half_c), 1) + reach, taps, 1)
    colt_ref[...] = pick(iota((half_c, cols), 1) - 2 * iota((half_c, cols), 0) + reach, taps, 1)
    for g in range(tiles // chunk):
        field = field_ref[g * fr : (g + 1) * fr, :]
        blurred = jnp.dot(row_bd, field, preferred_element_type=jnp.float32).astype(jnp.bfloat16)
        pred_ref[g * fh : (g + 1) * fh, :] = jnp.dot(
            blurred, col, preferred_element_type=jnp.float32
        ).astype(jnp.bfloat16)
    pad[...] = jnp.zeros(pad.shape, jnp.int32)
    pad[:, :n_words] = words_ref[...]
    per_row = half_c // 2 // 32
    for t in range(tiles):
        words = jnp.broadcast_to(pad[t : t + 1, :], (8, 128))
        for i0 in range(0, half_r, 8):
            for j0 in range(0, half_c, 128):
                i = iota((8, 128), 0) + i0
                j = iota((8, 128), 1) + j0
                word = jnp.take_along_axis(words, i // 2 * per_row + j // 64, axis=1)
                bit = jnp.bitwise_and(jnp.right_shift(word, j // 2 % 32), 1)
                valid_ref[t * half_r + i0 : t * half_r + i0 + 8, j0 : j0 + 128] = bit.astype(jnp.float32)


def after(sizes, ring, owners_ref, pred_ref, valid_ref, colt_ref, rowt_ref, own_ref, *refs):
    tiles, chunk, members, rows, cols = sizes
    n_tile, n_mem = ring
    per = n_tile // n_mem
    half_r, half_c = rows // 2, cols // 2
    arrived, out_ref, scenes = refs[:n_tile], refs[n_tile], refs[n_tile + 1]
    fields = chunk * members
    fr, fh = fields * rows, fields * half_r
    here, member = lax.axis_index("tile"), lax.axis_index("member")
    for p in range(n_tile):
        scenes[p] = arrived[p][...]
    scenes[n_tile] = own_ref[...]
    owner = [owners_ref[0, t] for t in range(tiles)]
    for g in range(tiles // chunk):
        parts = []
        for t in range(g * chunk, (g + 1) * chunk):
            rank = 0
            for u in range(t):
                rank = rank + jnp.where(owner[u] == owner[t], 1, 0)
            k = (here - owner[t]) % per
            j = (member - owner[t] // per) % n_mem
            mine = jnp.logical_and(owner[t] == here, here // per == member)
            step = jnp.where(mine, n_tile, k * n_mem + j)
            seen = scenes[step, 0, rank].astype(jnp.float32)
            sigma = scenes[step, 1, rank].astype(jnp.float32)
            weight = valid_ref[t * half_r : (t + 1) * half_r, :] / (sigma * sigma)
            for m in range(members):
                at = (t * members + m) * half_r
                gap = seen - pred_ref[at : at + half_r, :].astype(jnp.float32)
                parts.append((gap * weight).astype(jnp.bfloat16))
        misfit = jnp.concatenate(parts, axis=0)
        spread = jnp.dot(misfit, colt_ref[...], preferred_element_type=jnp.float32).astype(jnp.bfloat16)
        out_ref[g * fr : (g + 1) * fr, :] = jnp.dot(
            rowt_ref[...], spread, preferred_element_type=jnp.float32
        ).astype(jnp.bfloat16)


def per_device(sim_lai, owner_ids, cloud_words, scene_lai, scene_sigma, mtf_taps):
    n_tile, n_mem = lax.axis_size("tile"), lax.axis_size("member")
    _, tiles, members, rows, cols = sim_lai.shape
    half_r, half_c = rows // 2, cols // 2
    per = n_tile // n_mem
    both = jnp.stack([scene_lai[0, 0], scene_sigma[0, 0]], 0)
    here = lax.axis_index("tile")
    blocks = [lax.dynamic_slice_in_dim(both, (here + k) % per * CAP, CAP, 1) for k in range(per)]
    own = blocks[0]
    arrived = [lax.ppermute(blocks[k], GROUP, pairs) for k, j, pairs in plan(n_tile, n_mem)]
    arrived = [pltpu.with_memory_space_constraint(x, pltpu.VMEM) for x in arrived]
    chunk = chunk_tiles(tiles, members, rows)
    sizes = (tiles, chunk, members, rows, cols)
    fields = chunk * members
    fr, fh = fields * rows, fields * half_r
    vmem = pl.BlockSpec(memory_space=pltpu.VMEM)
    smem = pl.BlockSpec(memory_space=pltpu.SMEM)
    pred, valid, colt, rowt = pl.pallas_call(
        lambda *refs: before(sizes, *refs),
        out_shape=(
            pltpu.VMEM((tiles * members * half_r, half_c), jnp.bfloat16),
            pltpu.VMEM((tiles * half_r, half_c), jnp.float32),
            pltpu.VMEM((half_c, cols), jnp.bfloat16),
            pltpu.VMEM((fr, fh), jnp.bfloat16),
        ),
        in_specs=[vmem] * 3,
        out_specs=[vmem] * 4,
        scratch_shapes=[pltpu.VMEM((tiles, 128), jnp.int32)],
        name="before",
    )(mtf_taps, cloud_words[0], sim_lai.reshape(tiles * members * rows, cols))
    resident = [pltpu.with_memory_space_constraint(x, pltpu.VMEM) for x in (pred, valid, colt, rowt, own)]
    out = pl.pallas_call(
        lambda *refs: after(sizes, (n_tile, n_mem), *refs),
        out_shape=jax.ShapeDtypeStruct((tiles * members * rows, cols), jnp.bfloat16),
        in_specs=[smem] + [vmem] * (5 + n_tile),
        out_specs=vmem,
        scratch_shapes=[pltpu.VMEM((n_tile + 1, 2, CAP, half_r, half_c), jnp.bfloat16)],
        name="after",
    )(owner_ids, *resident, *arrived)
    return out.reshape(sim_lai.shape)


def solution(mesh):
    placed = (
        P("date", ("region", "tile"), "member", None, None),
        P("date", ("region", "tile")),
        P("date", ("region", "tile"), None),
        P("date", ("region", "tile"), "member", None, None),
        P("date", ("region", "tile"), "member", None, None),
        P(),
    )
    return jax.shard_map(
        per_device,
        mesh=mesh,
        in_specs=placed,
        out_specs=P("date", ("region", "tile"), "member", None, None),
        check_vma=False,
    )
```

```python
import jax
import jax.numpy as jnp
from jax import lax
from jax.experimental import pallas as pl
from jax.experimental.pallas import tpu as pltpu
from jax.sharding import PartitionSpec as P

CAP = 2
GROUP = ("tile", "member")


TUNED = {
    (4, 2): (
        (2, 6, 3, 4, 0, 7, 1, 5),
        (2, 5, 0, 7, 1, 6, 3, 4),
        (1, 7, 0, 6, 3, 4, 2, 5),
        (3, 4, 1, 5, 2, 7, 0, 6),
    ),
}


def plan(n_tile, n_mem):
    if (n_tile, n_mem) in TUNED:
        return TUNED[n_tile, n_mem]
    per = n_tile // n_mem
    steps = []
    for k in range(per):
        for j in range(n_mem):
            to = [
                (mm * per + (o + k) % per) * n_mem + (o // per + j) % n_mem
                for o in range(n_tile)
                for mm in range(n_mem)
            ]
            idle = [d for d, t in enumerate(to) if d == t]
            for d, t in zip(idle, idle[1:] + idle[:1]):
                to[d] = t
            steps.append(tuple(to))
    return tuple(steps)


def serves(n_tile, n_mem, device, target):
    per = n_tile // n_mem
    mm, s = device % n_mem, target // n_mem
    return s % per if s // per == mm else None


def packed(values, width, index):
    word = sum(v << (width * i) for i, v in enumerate(values))
    return jnp.bitwise_and(jnp.right_shift(jnp.int32(word), index * width), (1 << width) - 1)


def sent_block(n_tile, n_mem, step, to):
    per = n_tile // n_mem
    here, member = lax.axis_index("tile"), lax.axis_index("member")
    if (n_tile, n_mem) not in TUNED:
        return (here + step // n_mem) % per
    width = max(1, (per - 1).bit_length())
    sources = [serves(n_tile, n_mem, d, t) or 0 for d, t in enumerate(to)]
    return packed(sources, width, here * n_mem + member)


def arrival(n_tile, n_mem, owner):
    per = n_tile // n_mem
    here, member = lax.axis_index("tile"), lax.axis_index("member")
    if (n_tile, n_mem) in TUNED:
        device = here * n_mem + member
        steps = TUNED[n_tile, n_mem]
        width = n_tile.bit_length()
        out = jnp.int32(0)
        for o in range(n_tile):
            came = []
            for d in range(n_tile * n_mem):
                holder = o * n_mem + d // n_mem // per
                came.append(n_tile if holder == d else [to[holder] for to in steps].index(d))
            out = jnp.where(owner == o, packed(came, width, device), out)
        return out
    k, j = (here - owner) % per, (member - owner // per) % n_mem
    mine = jnp.logical_and(owner == here, here // per == member)
    return jnp.where(mine, n_tile, k * n_mem + j)


def chunk_tiles(tiles, members, rows):
    best = 1
    for c in range(1, tiles + 1):
        if tiles % c == 0 and c * members * rows <= 256:
            best = c
    return best


def iota(shape, dim):
    return lax.broadcasted_iota(jnp.int32, shape, dim)


def pick(which, taps, row):
    out = jnp.zeros(which.shape, jnp.float32)
    for k in range(taps.shape[1]):
        out = jnp.where(which == k, taps[row : row + 1, k : k + 1], out)
    return out.astype(jnp.bfloat16)


def before(sizes, taps_ref, words_ref, field_ref, pred_ref, valid_ref, colt_ref, rowt_ref, pad):
    tiles, chunk, members, rows, cols = sizes
    half_r, half_c = rows // 2, cols // 2
    n_words = words_ref.shape[1]
    taps = taps_ref[...]
    taps = taps / jnp.sum(taps, axis=1, keepdims=True)
    reach = taps.shape[1] // 2
    fields = chunk * members
    fr, fh = fields * rows, fields * half_r
    i, r = iota((fh, fr), 0), iota((fh, fr), 1)
    row_bd = jnp.where(
        i // half_r == r // rows, r % rows - 2 * (i % half_r) + reach, -1
    )
    row_bd = pick(row_bd, taps, 0)
    i, r = iota((fr, fh), 1), iota((fr, fh), 0)
    rowt = jnp.where(i // half_r == r // rows, r % rows - 2 * (i % half_r) + reach, -1)
    rowt_ref[...] = pick(rowt, taps, 0)
    col = pick(iota((cols, half_c), 0) - 2 * iota((cols, half_c), 1) + reach, taps, 1)
    colt_ref[...] = pick(iota((half_c, cols), 1) - 2 * iota((half_c, cols), 0) + reach, taps, 1)
    for g in range(tiles // chunk):
        field = field_ref[g * fr : (g + 1) * fr, :]
        blurred = jnp.dot(row_bd, field, preferred_element_type=jnp.float32).astype(jnp.bfloat16)
        pred_ref[g * fh : (g + 1) * fh, :] = jnp.dot(
            blurred, col, preferred_element_type=jnp.float32
        ).astype(jnp.bfloat16)
    pad[...] = jnp.zeros(pad.shape, jnp.int32)
    pad[:, :n_words] = words_ref[...]
    per_row = half_c // 2 // 32
    for t in range(tiles):
        words = jnp.broadcast_to(pad[t : t + 1, :], (8, 128))
        for i0 in range(0, half_r, 8):
            for j0 in range(0, half_c, 128):
                i = iota((8, 128), 0) + i0
                j = iota((8, 128), 1) + j0
                word = jnp.take_along_axis(words, i // 2 * per_row + j // 64, axis=1)
                bit = jnp.bitwise_and(jnp.right_shift(word, j // 2 % 32), 1)
                valid_ref[t * half_r + i0 : t * half_r + i0 + 8, j0 : j0 + 128] = bit.astype(jnp.float32)


def after(sizes, ring, owners_ref, pred_ref, valid_ref, colt_ref, rowt_ref, own_ref, *refs):
    tiles, chunk, members, rows, cols = sizes
    n_tile, n_mem = ring
    half_r, half_c = rows // 2, cols // 2
    arrived, out_ref, scenes = refs[:n_tile], refs[n_tile], refs[n_tile + 1]
    fields = chunk * members
    fr, fh = fields * rows, fields * half_r
    for p in range(n_tile):
        scenes[p] = arrived[p][...]
    scenes[n_tile] = own_ref[...]
    owner = [owners_ref[0, t] for t in range(tiles)]
    for g in range(tiles // chunk):
        parts = []
        for t in range(g * chunk, (g + 1) * chunk):
            rank = 0
            for u in range(t):
                rank = rank + jnp.where(owner[u] == owner[t], 1, 0)
            step = arrival(n_tile, n_mem, owner[t])
            seen = scenes[step, 0, rank].astype(jnp.float32)
            sigma = scenes[step, 1, rank].astype(jnp.float32)
            weight = valid_ref[t * half_r : (t + 1) * half_r, :] / (sigma * sigma)
            for m in range(members):
                at = (t * members + m) * half_r
                gap = seen - pred_ref[at : at + half_r, :].astype(jnp.float32)
                parts.append((gap * weight).astype(jnp.bfloat16))
        misfit = jnp.concatenate(parts, axis=0)
        spread = jnp.dot(misfit, colt_ref[...], preferred_element_type=jnp.float32).astype(jnp.bfloat16)
        out_ref[g * fr : (g + 1) * fr, :] = jnp.dot(
            rowt_ref[...], spread, preferred_element_type=jnp.float32
        ).astype(jnp.bfloat16)


def per_device(sim_lai, owner_ids, cloud_words, scene_lai, scene_sigma, mtf_taps):
    n_tile, n_mem = lax.axis_size("tile"), lax.axis_size("member")
    _, tiles, members, rows, cols = sim_lai.shape
    half_r, half_c = rows // 2, cols // 2
    per = n_tile // n_mem
    both = jnp.stack([scene_lai[0, 0], scene_sigma[0, 0]], 0)
    own = lax.dynamic_slice_in_dim(both, lax.axis_index("tile") % per * CAP, CAP, 1)
    steps = plan(n_tile, n_mem)
    arrived = []
    for p in range(n_tile):
        block = lax.dynamic_slice_in_dim(both, sent_block(n_tile, n_mem, p, steps[p]) * CAP, CAP, 1)
        arrived.append(lax.ppermute(block, GROUP, list(enumerate(steps[p]))))
    arrived = [pltpu.with_memory_space_constraint(x, pltpu.VMEM) for x in arrived]
    chunk = chunk_tiles(tiles, members, rows)
    sizes = (tiles, chunk, members, rows, cols)
    fields = chunk * members
    fr, fh = fields * rows, fields * half_r
    vmem = pl.BlockSpec(memory_space=pltpu.VMEM)
    smem = pl.BlockSpec(memory_space=pltpu.SMEM)
    pred, valid, colt, rowt = pl.pallas_call(
        lambda *refs: before(sizes, *refs),
        out_shape=(
            pltpu.VMEM((tiles * members * half_r, half_c), jnp.bfloat16),
            pltpu.VMEM((tiles * half_r, half_c), jnp.float32),
            pltpu.VMEM((half_c, cols), jnp.bfloat16),
            pltpu.VMEM((fr, fh), jnp.bfloat16),
        ),
        in_specs=[vmem] * 3,
        out_specs=[vmem] * 4,
        scratch_shapes=[pltpu.VMEM((tiles, 128), jnp.int32)],
        name="before",
    )(mtf_taps, cloud_words[0], sim_lai.reshape(tiles * members * rows, cols))
    resident = [pltpu.with_memory_space_constraint(x, pltpu.VMEM) for x in (pred, valid, colt, rowt, own)]
    out = pl.pallas_call(
        lambda *refs: after(sizes, (n_tile, n_mem), *refs),
        out_shape=jax.ShapeDtypeStruct((tiles * members * rows, cols), jnp.bfloat16),
        in_specs=[smem] + [vmem] * (5 + n_tile),
        out_specs=vmem,
        scratch_shapes=[pltpu.VMEM((n_tile + 1, 2, CAP, half_r, half_c), jnp.bfloat16)],
        name="after",
    )(owner_ids, *resident, *arrived)
    return out.reshape(sim_lai.shape)


def solution(mesh):
    placed = (
        P("date", ("region", "tile"), "member", None, None),
        P("date", ("region", "tile")),
        P("date", ("region", "tile"), None),
        P("date", ("region", "tile"), "member", None, None),
        P("date", ("region", "tile"), "member", None, None),
        P(),
    )
    return jax.shard_map(
        per_device,
        mesh=mesh,
        in_specs=placed,
        out_specs=P("date", ("region", "tile"), "member", None, None),
        check_vma=False,
    )
```

```python
import jax
import jax.numpy as jnp
from jax import lax
from jax.experimental import pallas as pl
from jax.experimental.pallas import tpu as pltpu
from jax.sharding import PartitionSpec as P

CAP = 2
PIECES = 2
GROUP = ("tile", "member")


TUNED = {
    (4, 2): (
        (3, 6, 1, 7, 0, 4, 2, 5),
        (5, 4, 0, 6, 3, 7, 1, 2),
        (2, 7, 0, 5, 1, 6, 3, 4),
        (1, 5, 3, 4, 2, 7, 0, 6),
    ),
}


def plan(n_tile, n_mem):
    if (n_tile, n_mem) in TUNED:
        return TUNED[n_tile, n_mem]
    per = n_tile // n_mem
    steps = []
    for k in range(per):
        for j in range(n_mem):
            to = [
                (mm * per + (o + k) % per) * n_mem + (o // per + j) % n_mem
                for o in range(n_tile)
                for mm in range(n_mem)
            ]
            idle = [d for d, t in enumerate(to) if d == t]
            for d, t in zip(idle, idle[1:] + idle[:1]):
                to[d] = t
            steps.append(tuple(to))
    return tuple(steps)


def serves(n_tile, n_mem, device, target):
    per = n_tile // n_mem
    mm, s = device % n_mem, target // n_mem
    return s % per if s // per == mm else None


def packed(values, width, index):
    word = sum(v << (width * i) for i, v in enumerate(values))
    return jnp.bitwise_and(jnp.right_shift(jnp.int32(word), index * width), (1 << width) - 1)


def sent_block(n_tile, n_mem, step, to):
    per = n_tile // n_mem
    here, member = lax.axis_index("tile"), lax.axis_index("member")
    if (n_tile, n_mem) not in TUNED:
        return (here + step // n_mem) % per
    width = max(1, (per - 1).bit_length())
    sources = [serves(n_tile, n_mem, d, t) or 0 for d, t in enumerate(to)]
    return packed(sources, width, here * n_mem + member)


def arrival(n_tile, n_mem, owner):
    per = n_tile // n_mem
    here, member = lax.axis_index("tile"), lax.axis_index("member")
    if (n_tile, n_mem) in TUNED:
        device = here * n_mem + member
        steps = TUNED[n_tile, n_mem]
        width = n_tile.bit_length()
        out = jnp.int32(0)
        for o in range(n_tile):
            came = []
            for d in range(n_tile * n_mem):
                holder = o * n_mem + d // n_mem // per
                came.append(n_tile if holder == d else [to[holder] for to in steps].index(d))
            out = jnp.where(owner == o, packed(came, width, device), out)
        return out
    k, j = (here - owner) % per, (member - owner // per) % n_mem
    mine = jnp.logical_and(owner == here, here // per == member)
    return jnp.where(mine, n_tile, k * n_mem + j)


def chunk_tiles(tiles, members, rows):
    best = 1
    for c in range(1, tiles + 1):
        if tiles % c == 0 and c * members * rows <= 256:
            best = c
    return best


def iota(shape, dim):
    return lax.broadcasted_iota(jnp.int32, shape, dim)


def pick(which, taps, row):
    out = jnp.zeros(which.shape, jnp.float32)
    for k in range(taps.shape[1]):
        out = jnp.where(which == k, taps[row : row + 1, k : k + 1], out)
    return out.astype(jnp.bfloat16)


def before(sizes, ring, owners_ref, taps_ref, words_ref, field_ref, pred_ref, valid_ref, colt_ref, rowt_ref, pick_ref, pad):
    tiles, chunk, members, rows, cols = sizes
    half_r, half_c = rows // 2, cols // 2
    n_words = words_ref.shape[1]
    owner = [owners_ref[0, t] for t in range(tiles)]
    for t in range(tiles):
        rank = 0
        for u in range(t):
            rank = rank + jnp.where(owner[u] == owner[t], 1, 0)
        pick_ref[t] = arrival(*ring, owner[t]) * CAP + rank
    taps = taps_ref[...]
    taps = taps / jnp.sum(taps, axis=1, keepdims=True)
    reach = taps.shape[1] // 2
    fields = chunk * members
    fr, fh = fields * rows, fields * half_r
    i, r = iota((fh, fr), 0), iota((fh, fr), 1)
    row_bd = jnp.where(
        i // half_r == r // rows, r % rows - 2 * (i % half_r) + reach, -1
    )
    row_bd = pick(row_bd, taps, 0)
    i, r = iota((fr, fh), 1), iota((fr, fh), 0)
    rowt = jnp.where(i // half_r == r // rows, r % rows - 2 * (i % half_r) + reach, -1)
    rowt_ref[...] = pick(rowt, taps, 0)
    col = pick(iota((cols, half_c), 0) - 2 * iota((cols, half_c), 1) + reach, taps, 1)
    colt_ref[...] = pick(iota((half_c, cols), 1) - 2 * iota((half_c, cols), 0) + reach, taps, 1)
    for g in range(tiles // chunk):
        field = field_ref[g * fr : (g + 1) * fr, :]
        blurred = jnp.dot(row_bd, field, preferred_element_type=jnp.float32).astype(jnp.bfloat16)
        pred_ref[g * fh : (g + 1) * fh, :] = jnp.dot(
            blurred, col, preferred_element_type=jnp.float32
        ).astype(jnp.bfloat16)
    pad[...] = jnp.zeros(pad.shape, jnp.int32)
    pad[:, :n_words] = words_ref[...]
    per_row = half_c // 2 // 32
    for t in range(tiles):
        words = jnp.broadcast_to(pad[t : t + 1, :], (8, 128))
        for i0 in range(0, half_r, 8):
            for j0 in range(0, half_c, 128):
                i = iota((8, 128), 0) + i0
                j = iota((8, 128), 1) + j0
                word = jnp.take_along_axis(words, i // 2 * per_row + j // 64, axis=1)
                bit = jnp.bitwise_and(jnp.right_shift(word, j // 2 % 32), 1)
                valid_ref[t * half_r + i0 : t * half_r + i0 + 8, j0 : j0 + 128] = bit.astype(jnp.float32)


def after(sizes, n_tile, pick_ref, pred_ref, valid_ref, colt_ref, rowt_ref, own_ref, *refs):
    tiles, chunk, members, rows, cols = sizes
    half_r, half_c = rows // 2, cols // 2
    arrived, out_ref, scenes, update, sems = refs[:n_tile], refs[n_tile], *refs[n_tile + 1 :]
    fields = chunk * members
    fr, fh = fields * rows, fields * half_r
    for p, block in enumerate((*arrived, own_ref)):
        for r in range(CAP):
            for kind in range(2):
                scenes[p * CAP + r, kind] = block[kind, r]
    cuts = PIECES if fields % PIECES == 0 else 1
    pr, ph = fr // cuts, fh // cuts
    copies = []
    for g in range(tiles // chunk):
        parts = []
        for t in range(g * chunk, (g + 1) * chunk):
            seen = scenes[pick_ref[t], 0].astype(jnp.float32)
            sigma = scenes[pick_ref[t], 1].astype(jnp.float32)
            weight = valid_ref[t * half_r : (t + 1) * half_r, :] / (sigma * sigma)
            for m in range(members):
                at = (t * members + m) * half_r
                gap = seen - pred_ref[at : at + half_r, :].astype(jnp.float32)
                parts.append((gap * weight).astype(jnp.bfloat16))
        misfit = jnp.concatenate(parts, axis=0)
        spread = jnp.dot(misfit, colt_ref[...], preferred_element_type=jnp.float32).astype(jnp.bfloat16)
        for c in range(cuts):
            at = pl.ds(g * fr + c * pr, pr)
            update[at, :] = jnp.dot(
                rowt_ref[:pr, :ph], spread[c * ph : (c + 1) * ph, :], preferred_element_type=jnp.float32
            ).astype(jnp.bfloat16)
            copies.append(pltpu.make_async_copy(update.at[at, :], out_ref.at[at, :], sems.at[len(copies)]))
            copies[-1].start()
    for copy in copies:
        copy.wait()


def per_device(sim_lai, owner_ids, cloud_words, scene_lai, scene_sigma, mtf_taps):
    n_tile, n_mem = lax.axis_size("tile"), lax.axis_size("member")
    _, tiles, members, rows, cols = sim_lai.shape
    half_r, half_c = rows // 2, cols // 2
    per = n_tile // n_mem
    both = jnp.stack([scene_lai[0, 0], scene_sigma[0, 0]], 0)
    own = lax.dynamic_slice_in_dim(both, lax.axis_index("tile") % per * CAP, CAP, 1)
    steps = plan(n_tile, n_mem)
    arrived = []
    for p in range(n_tile):
        block = lax.dynamic_slice_in_dim(both, sent_block(n_tile, n_mem, p, steps[p]) * CAP, CAP, 1)
        arrived.append(lax.ppermute(block, GROUP, list(enumerate(steps[p]))))
    arrived = [pltpu.with_memory_space_constraint(x, pltpu.VMEM) for x in arrived]
    chunk = chunk_tiles(tiles, members, rows)
    sizes = (tiles, chunk, members, rows, cols)
    fields = chunk * members
    fr, fh = fields * rows, fields * half_r
    vmem = pl.BlockSpec(memory_space=pltpu.VMEM)
    smem = pl.BlockSpec(memory_space=pltpu.SMEM)
    pred, valid, colt, rowt, picks = pl.pallas_call(
        lambda *refs: before(sizes, (n_tile, n_mem), *refs),
        out_shape=(
            pltpu.VMEM((tiles * members * half_r, half_c), jnp.bfloat16),
            pltpu.VMEM((tiles * half_r, half_c), jnp.float32),
            pltpu.VMEM((half_c, cols), jnp.bfloat16),
            pltpu.VMEM((fr, fh), jnp.bfloat16),
            pltpu.SMEM((tiles,), jnp.int32),
        ),
        in_specs=[smem] + [vmem] * 3,
        out_specs=[vmem] * 4 + [smem],
        scratch_shapes=[pltpu.VMEM((tiles, 128), jnp.int32)],
        name="before",
    )(owner_ids, mtf_taps, cloud_words[0], sim_lai.reshape(tiles * members * rows, cols))
    resident = [pltpu.with_memory_space_constraint(x, pltpu.VMEM) for x in (pred, valid, colt, rowt, own)]
    picks = pltpu.with_memory_space_constraint(picks, pltpu.SMEM)
    out = pl.pallas_call(
        lambda *refs: after(sizes, n_tile, *refs),
        out_shape=jax.ShapeDtypeStruct((tiles * members * rows, cols), jnp.bfloat16),
        in_specs=[smem] + [vmem] * (5 + n_tile),
        out_specs=pl.BlockSpec(memory_space=pl.ANY),
        scratch_shapes=[
            pltpu.VMEM(((n_tile + 1) * CAP, 2, half_r, half_c), jnp.bfloat16),
            pltpu.VMEM((tiles * members * rows, cols), jnp.bfloat16),
            pltpu.SemaphoreType.DMA((PIECES * tiles // chunk,)),
        ],
        name="after",
    )(picks, *resident, *arrived)
    return out.reshape(sim_lai.shape)


def solution(mesh):
    placed = (
        P("date", ("region", "tile"), "member", None, None),
        P("date", ("region", "tile")),
        P("date", ("region", "tile"), None),
        P("date", ("region", "tile"), "member", None, None),
        P("date", ("region", "tile"), "member", None, None),
        P(),
    )
    return jax.shard_map(
        per_device,
        mesh=mesh,
        in_specs=placed,
        out_specs=P("date", ("region", "tile"), "member", None, None),
        check_vma=False,
    )
```

```python
import jax
import jax.numpy as jnp
from jax import lax
from jax.experimental import pallas as pl
from jax.experimental.pallas import tpu as pltpu
from jax.sharding import PartitionSpec as P

CAP = 2
PIECES = 2
GROUP = ("tile", "member", "date")


TUNED = {
    (4, 2): (
        (1, 5, 3, 6, 0, 4, 2, 7),
        (2, 6, 0, 5, 3, 7, 1, 4),
        (0, 7, 1, 4, 2, 6, 3, 5),
        (3, 4, 2, 7, 1, 5, 0, 6),
    ),
}


def plan(n_tile, n_mem):
    if (n_tile, n_mem) in TUNED:
        return TUNED[n_tile, n_mem]
    per = n_tile // n_mem
    steps = []
    for k in range(per):
        for j in range(n_mem):
            to = [
                (mm * per + (o + k) % per) * n_mem + (o // per + j) % n_mem
                for o in range(n_tile)
                for mm in range(n_mem)
            ]
            steps.append(tuple(to))
    return tuple(steps)


def pairs(to, n_date):
    return [
        (src * n_date + d, dst * n_date + (d if src != dst else (d + 1) % n_date))
        for src, dst in enumerate(to)
        for d in range(n_date)
    ]


def packed(values, width, index):
    word = sum(v << (width * i) for i, v in enumerate(values))
    return jnp.bitwise_and(jnp.right_shift(jnp.int32(word), index * width), (1 << width) - 1)


def sent_block(n_tile, n_mem, step, to):
    per = n_tile // n_mem
    here, member = lax.axis_index("tile"), lax.axis_index("member")
    if (n_tile, n_mem) not in TUNED:
        return (here + step // n_mem) % per
    width = max(1, (per - 1).bit_length())
    sources = [t // n_mem % per for t in to]
    return packed(sources, width, here * n_mem + member)


def arrival(n_tile, n_mem, owner):
    per = n_tile // n_mem
    here, member = lax.axis_index("tile"), lax.axis_index("member")
    if (n_tile, n_mem) in TUNED:
        device = here * n_mem + member
        steps = TUNED[n_tile, n_mem]
        width = n_tile.bit_length()
        out = jnp.int32(0)
        for o in range(n_tile):
            came = []
            for d in range(n_tile * n_mem):
                holder = o * n_mem + d // n_mem // per
                came.append(n_tile if holder == d else [to[holder] for to in steps].index(d))
            out = jnp.where(owner == o, packed(came, width, device), out)
        return out
    k, j = (here - owner) % per, (member - owner // per) % n_mem
    mine = jnp.logical_and(owner == here, here // per == member)
    return jnp.where(mine, n_tile, k * n_mem + j)


def chunk_tiles(tiles, members, rows):
    best = 1
    for c in range(1, tiles + 1):
        if tiles % c == 0 and c * members * rows <= 256:
            best = c
    return best


def iota(shape, dim):
    return lax.broadcasted_iota(jnp.int32, shape, dim)


def pick(which, taps, row):
    out = jnp.zeros(which.shape, jnp.float32)
    for k in range(taps.shape[1]):
        out = jnp.where(which == k, taps[row : row + 1, k : k + 1], out)
    return out.astype(jnp.bfloat16)


def before(sizes, ring, owners_ref, taps_ref, words_ref, field_ref, pred_ref, valid_ref, colt_ref, rowt_ref, pick_ref, pad):
    tiles, chunk, members, rows, cols = sizes
    half_r, half_c = rows // 2, cols // 2
    n_words = words_ref.shape[1]
    owner = [owners_ref[0, t] for t in range(tiles)]
    for t in range(tiles):
        rank = 0
        for u in range(t):
            rank = rank + jnp.where(owner[u] == owner[t], 1, 0)
        pick_ref[t] = arrival(*ring, owner[t]) * CAP + rank
    taps = taps_ref[...]
    taps = taps / jnp.sum(taps, axis=1, keepdims=True)
    reach = taps.shape[1] // 2
    fields = chunk * members
    fr, fh = fields * rows, fields * half_r
    i, r = iota((fh, fr), 0), iota((fh, fr), 1)
    row_bd = jnp.where(
        i // half_r == r // rows, r % rows - 2 * (i % half_r) + reach, -1
    )
    row_bd = pick(row_bd, taps, 0)
    i, r = iota((fr, fh), 1), iota((fr, fh), 0)
    rowt = jnp.where(i // half_r == r // rows, r % rows - 2 * (i % half_r) + reach, -1)
    rowt_ref[...] = pick(rowt, taps, 0)
    col = pick(iota((cols, half_c), 0) - 2 * iota((cols, half_c), 1) + reach, taps, 1)
    colt_ref[...] = pick(iota((half_c, cols), 1) - 2 * iota((half_c, cols), 0) + reach, taps, 1)
    for g in range(tiles // chunk):
        field = field_ref[g * fr : (g + 1) * fr, :]
        blurred = jnp.dot(row_bd, field, preferred_element_type=jnp.float32).astype(jnp.bfloat16)
        pred_ref[g * fh : (g + 1) * fh, :] = jnp.dot(
            blurred, col, preferred_element_type=jnp.float32
        ).astype(jnp.bfloat16)
    pad[...] = jnp.zeros(pad.shape, jnp.int32)
    pad[:, :n_words] = words_ref[...]
    per_row = half_c // 2 // 32
    for t in range(tiles):
        words = jnp.broadcast_to(pad[t : t + 1, :], (8, 128))
        for i0 in range(0, half_r, 8):
            for j0 in range(0, half_c, 128):
                i = iota((8, 128), 0) + i0
                j = iota((8, 128), 1) + j0
                word = jnp.take_along_axis(words, i // 2 * per_row + j // 64, axis=1)
                bit = jnp.bitwise_and(jnp.right_shift(word, j // 2 % 32), 1)
                valid_ref[t * half_r + i0 : t * half_r + i0 + 8, j0 : j0 + 128] = bit.astype(jnp.float32)


def after(sizes, n_tile, pick_ref, pred_ref, valid_ref, colt_ref, rowt_ref, own_ref, *refs):
    tiles, chunk, members, rows, cols = sizes
    half_r, half_c = rows // 2, cols // 2
    arrived, out_ref, scenes, update, sems = refs[:n_tile], refs[n_tile], *refs[n_tile + 1 :]
    fields = chunk * members
    fr, fh = fields * rows, fields * half_r
    for p, block in enumerate((*arrived, own_ref)):
        for r in range(CAP):
            for kind in range(2):
                scenes[p * CAP + r, kind] = block[kind, r]
    cuts = PIECES if fields % PIECES == 0 else 1
    pr, ph = fr // cuts, fh // cuts
    copies = []
    for g in range(tiles // chunk):
        parts = []
        for t in range(g * chunk, (g + 1) * chunk):
            seen = scenes[pick_ref[t], 0].astype(jnp.float32)
            sigma = scenes[pick_ref[t], 1].astype(jnp.float32)
            weight = valid_ref[t * half_r : (t + 1) * half_r, :] / (sigma * sigma)
            for m in range(members):
                at = (t * members + m) * half_r
                gap = seen - pred_ref[at : at + half_r, :].astype(jnp.float32)
                parts.append((gap * weight).astype(jnp.bfloat16))
        misfit = jnp.concatenate(parts, axis=0)
        spread = jnp.dot(misfit, colt_ref[...], preferred_element_type=jnp.float32).astype(jnp.bfloat16)
        for c in range(cuts):
            at = pl.ds(g * fr + c * pr, pr)
            update[at, :] = jnp.dot(
                rowt_ref[:pr, :ph], spread[c * ph : (c + 1) * ph, :], preferred_element_type=jnp.float32
            ).astype(jnp.bfloat16)
            copies.append(pltpu.make_async_copy(update.at[at, :], out_ref.at[at, :], sems.at[len(copies)]))
            copies[-1].start()
    for copy in copies:
        copy.wait()


def per_device(sim_lai, owner_ids, cloud_words, scene_lai, scene_sigma, mtf_taps):
    n_tile, n_mem = lax.axis_size("tile"), lax.axis_size("member")
    _, tiles, members, rows, cols = sim_lai.shape
    half_r, half_c = rows // 2, cols // 2
    per = n_tile // n_mem
    both = jnp.stack([scene_lai[0, 0], scene_sigma[0, 0]], 0)
    own = lax.dynamic_slice_in_dim(both, lax.axis_index("tile") % per * CAP, CAP, 1)
    steps = plan(n_tile, n_mem)
    arrived = []
    for p in range(n_tile):
        block = lax.dynamic_slice_in_dim(both, sent_block(n_tile, n_mem, p, steps[p]) * CAP, CAP, 1)
        arrived.append(lax.ppermute(block, GROUP, pairs(steps[p], lax.axis_size("date"))))
    arrived = [pltpu.with_memory_space_constraint(x, pltpu.VMEM) for x in arrived]
    chunk = chunk_tiles(tiles, members, rows)
    sizes = (tiles, chunk, members, rows, cols)
    fields = chunk * members
    fr, fh = fields * rows, fields * half_r
    vmem = pl.BlockSpec(memory_space=pltpu.VMEM)
    smem = pl.BlockSpec(memory_space=pltpu.SMEM)
    pred, valid, colt, rowt, picks = pl.pallas_call(
        lambda *refs: before(sizes, (n_tile, n_mem), *refs),
        out_shape=(
            pltpu.VMEM((tiles * members * half_r, half_c), jnp.bfloat16),
            pltpu.VMEM((tiles * half_r, half_c), jnp.float32),
            pltpu.VMEM((half_c, cols), jnp.bfloat16),
            pltpu.VMEM((fr, fh), jnp.bfloat16),
            pltpu.SMEM((tiles,), jnp.int32),
        ),
        in_specs=[smem] + [vmem] * 3,
        out_specs=[vmem] * 4 + [smem],
        scratch_shapes=[pltpu.VMEM((tiles, 128), jnp.int32)],
        name="before",
    )(owner_ids, mtf_taps, cloud_words[0], sim_lai.reshape(tiles * members * rows, cols))
    resident = [pltpu.with_memory_space_constraint(x, pltpu.VMEM) for x in (pred, valid, colt, rowt, own)]
    picks = pltpu.with_memory_space_constraint(picks, pltpu.SMEM)
    out = pl.pallas_call(
        lambda *refs: after(sizes, n_tile, *refs),
        out_shape=jax.ShapeDtypeStruct((tiles * members * rows, cols), jnp.bfloat16),
        in_specs=[smem] + [vmem] * (5 + n_tile),
        out_specs=pl.BlockSpec(memory_space=pl.ANY),
        scratch_shapes=[
            pltpu.VMEM(((n_tile + 1) * CAP, 2, half_r, half_c), jnp.bfloat16),
            pltpu.VMEM((tiles * members * rows, cols), jnp.bfloat16),
            pltpu.SemaphoreType.DMA((PIECES * tiles // chunk,)),
        ],
        name="after",
    )(picks, *resident, *arrived)
    return out.reshape(sim_lai.shape)


def solution(mesh):
    placed = (
        P("date", ("region", "tile"), "member", None, None),
        P("date", ("region", "tile")),
        P("date", ("region", "tile"), None),
        P("date", ("region", "tile"), "member", None, None),
        P("date", ("region", "tile"), "member", None, None),
        P(),
    )
    return jax.shard_map(
        per_device,
        mesh=mesh,
        in_specs=placed,
        out_specs=P("date", ("region", "tile"), "member", None, None),
        check_vma=False,
    )
```

```python
import jax
import jax.numpy as jnp
from jax import lax
from jax.experimental import pallas as pl
from jax.experimental.pallas import tpu as pltpu
from jax.sharding import PartitionSpec as P

CAP = 2
PIECES = 2
GROUP = ("tile", "member", "date")


TUNED = {
    (4, 2): (
        (3, 4, 2, 6, 1, 5, 0, 7),
        (1, 5, 3, 7, 0, 4, 2, 6),
        (2, 6, 0, 5, 3, 7, 1, 4),
        (0, 7, 1, 4, 2, 6, 3, 5),
    ),
}


def plan(n_tile, n_mem):
    if (n_tile, n_mem) in TUNED:
        return TUNED[n_tile, n_mem]
    per = n_tile // n_mem
    steps = []
    for k in range(per):
        for j in range(n_mem):
            to = [
                (mm * per + (o + k) % per) * n_mem + (o // per + j) % n_mem
                for o in range(n_tile)
                for mm in range(n_mem)
            ]
            steps.append(tuple(to))
    return tuple(steps)


def pairs(to, n_date):
    return [
        (src * n_date + d, dst * n_date + (d if src != dst else (d + 1) % n_date))
        for src, dst in enumerate(to)
        for d in range(n_date)
    ]


def packed(values, width, index):
    word = sum(v << (width * i) for i, v in enumerate(values))
    return jnp.bitwise_and(jnp.right_shift(jnp.int32(word), index * width), (1 << width) - 1)


def sent_block(n_tile, n_mem, step, to):
    per = n_tile // n_mem
    here, member = lax.axis_index("tile"), lax.axis_index("member")
    if (n_tile, n_mem) not in TUNED:
        return (here + step // n_mem) % per
    width = max(1, (per - 1).bit_length())
    sources = [t // n_mem % per for t in to]
    return packed(sources, width, here * n_mem + member)


def arrival(n_tile, n_mem, owner):
    per = n_tile // n_mem
    here, member = lax.axis_index("tile"), lax.axis_index("member")
    if (n_tile, n_mem) in TUNED:
        device = here * n_mem + member
        steps = TUNED[n_tile, n_mem]
        width = n_tile.bit_length()
        out = jnp.int32(0)
        for o in range(n_tile):
            came = []
            for d in range(n_tile * n_mem):
                holder = o * n_mem + d // n_mem // per
                came.append(n_tile if holder == d else [to[holder] for to in steps].index(d))
            out = jnp.where(owner == o, packed(came, width, device), out)
        return out
    k, j = (here - owner) % per, (member - owner // per) % n_mem
    mine = jnp.logical_and(owner == here, here // per == member)
    return jnp.where(mine, n_tile, k * n_mem + j)


def chunk_tiles(tiles, members, rows):
    best = 1
    for c in range(1, tiles + 1):
        if tiles % c == 0 and c * members * rows <= 256:
            best = c
    return best


def iota(shape, dim):
    return lax.broadcasted_iota(jnp.int32, shape, dim)


def pack(steps, ring, scene_ref, sigma_ref, *outs):
    n_tile, n_mem = ring
    per = n_tile // n_mem
    blocks, (own_ref,) = outs[:n_tile], outs[n_tile:]
    for p in range(n_tile):
        at = pl.ds(sent_block(n_tile, n_mem, p, steps[p]) * CAP, CAP)
        blocks[p][0] = scene_ref[at]
        blocks[p][1] = sigma_ref[at]
    at = pl.ds(lax.axis_index("tile") % per * CAP, CAP)
    own_ref[0] = scene_ref[at]
    own_ref[1] = sigma_ref[at]


class Band:
    def __init__(self, taps, shape):
        self.taps = [jnp.broadcast_to(tap, shape) for tap in taps]
        self.shape, self.made = shape, {}
        self.row, self.lane = iota(shape, 0), iota(shape, 1)

    def tile(self, row_mul, lane_mul, offset, first=None, length=None):
        ends = [offset + r * row_mul * (self.shape[0] - 1) + c * lane_mul * (self.shape[1] - 1) for r in (0, 1) for c in (0, 1)]
        outside = max(ends) < 0 or min(ends) >= len(self.taps)
        if first is not None:
            outside = outside or first >= self.shape[1] or first + length <= 0
        key = None if outside else (row_mul, lane_mul, offset, first)
        if key not in self.made:
            out = jnp.zeros(self.shape, jnp.float32)
            if not outside:
                which = self.row * row_mul + self.lane * lane_mul + offset
                if first is not None:
                    inside = jnp.logical_and(self.lane >= first, self.lane < first + length)
                    which = jnp.where(inside, which, -1)
                for k, tap in enumerate(self.taps):
                    out = jnp.where(which == k, tap, out)
            self.made[key] = out.astype(jnp.bfloat16)
        return self.made[key]


def before(sizes, ring, owners_ref, taps_ref, words_ref, lai_ref, pred_ref, valid_ref, colt_ref, rowt_ref, pick_ref, *scratch):
    tiles, chunk, members, rows, cols = sizes
    half_r, half_c = rows // 2, cols // 2
    n_words = words_ref.shape[1]
    pad, col, rowd, field_ref, sem = scratch
    fetch = pltpu.make_async_copy(lai_ref, field_ref, sem)
    fetch.start()
    owner = [owners_ref[0, t] for t in range(tiles)]
    for t in range(tiles):
        rank = 0
        for u in range(t):
            rank = rank + jnp.where(owner[u] == owner[t], 1, 0)
        pick_ref[t] = arrival(*ring, owner[t]) * CAP + rank
    taps = taps_ref[...]
    taps = taps / jnp.sum(taps, axis=1, keepdims=True)
    reach = taps.shape[1] // 2
    fields = chunk * members
    fr, fh = fields * rows, fields * half_r
    high, wide = 16, 128
    down = Band([taps[0:1, k : k + 1] for k in range(taps.shape[1])], (high, wide))
    across = Band([taps[1:2, k : k + 1] for k in range(taps.shape[1])], (high, wide))
    for r in range(0, cols, high):
        for c in range(0, half_c, wide):
            col[r : r + high, c : c + wide] = across.tile(1, -2, r - 2 * c + reach)
    for r in range(0, half_c, high):
        for c in range(0, cols, wide):
            colt_ref[r : r + high, c : c + wide] = across.tile(-2, 1, c - 2 * r + reach)
    for r in range(0, fh, high):
        top = r // half_r * rows
        for c in range(0, fr, wide):
            rowd[r : r + high, c : c + wide] = down.tile(-2, 1, c - top - 2 * (r % half_r) + reach, top - c, rows)
    for r in range(0, rowt_ref.shape[0], high):
        left = r // rows * half_r
        width = min(wide, rowt_ref.shape[1])
        for c in range(0, rowt_ref.shape[1], width):
            tile = down.tile(1, -2, r % rows + 2 * (left - c) + reach, left - c, half_r)
            rowt_ref[r : r + high, c : c + width] = tile[:, :width]
    pad[...] = jnp.zeros(pad.shape, jnp.int32)
    pad[:, :n_words] = words_ref[...]
    per_row = half_c // 2 // 32
    for i0 in range(0, half_r, 8):
        for j0 in range(0, half_c, wide):
            i = iota((8, wide), 0) + i0
            j = iota((8, wide), 1) + j0
            which = jnp.right_shift(i, 1) * per_row + jnp.right_shift(j, 6)
            shift = jnp.bitwise_and(jnp.right_shift(j, 1), 31)
            for t in range(tiles):
                words = jnp.broadcast_to(pad[t : t + 1, :], (8, wide))
                word = jnp.take_along_axis(words, which, axis=1)
                bit = jnp.bitwise_and(jnp.right_shift(word, shift), 1)
                valid_ref[t * half_r + i0 : t * half_r + i0 + 8, j0 : j0 + wide] = bit.astype(jnp.float32)
    fetch.wait()
    for g in range(tiles // chunk):
        field = field_ref[g * fr : (g + 1) * fr, :]
        blurred = jnp.dot(rowd[...], field, preferred_element_type=jnp.float32).astype(jnp.bfloat16)
        pred_ref[g * fh : (g + 1) * fh, :] = jnp.dot(
            blurred, col[...], preferred_element_type=jnp.float32
        ).astype(jnp.bfloat16)


def after(sizes, n_tile, pick_ref, pred_ref, valid_ref, colt_ref, rowt_ref, own_ref, *refs):
    tiles, chunk, members, rows, cols = sizes
    half_r, half_c = rows // 2, cols // 2
    arrived, out_ref, scenes, update, sems = refs[:n_tile], refs[n_tile], *refs[n_tile + 1 :]
    fields = chunk * members
    fr, fh = fields * rows, fields * half_r
    for p, block in enumerate((*arrived, own_ref)):
        for r in range(CAP):
            for kind in range(2):
                scenes[p * CAP + r, kind] = block[kind, r]
    pr, ph = rowt_ref.shape
    cuts = fr // pr
    copies = []
    for g in range(tiles // chunk):
        parts = []
        for t in range(g * chunk, (g + 1) * chunk):
            seen = scenes[pick_ref[t], 0].astype(jnp.float32)
            sigma = scenes[pick_ref[t], 1].astype(jnp.float32)
            weight = valid_ref[t * half_r : (t + 1) * half_r, :] / (sigma * sigma)
            for m in range(members):
                at = (t * members + m) * half_r
                gap = seen - pred_ref[at : at + half_r, :].astype(jnp.float32)
                parts.append((gap * weight).astype(jnp.bfloat16))
        misfit = jnp.concatenate(parts, axis=0)
        spread = jnp.dot(misfit, colt_ref[...], preferred_element_type=jnp.float32).astype(jnp.bfloat16)
        for c in range(cuts):
            at = pl.ds(g * fr + c * pr, pr)
            update[at, :] = jnp.dot(
                rowt_ref[...], spread[c * ph : (c + 1) * ph, :], preferred_element_type=jnp.float32
            ).astype(jnp.bfloat16)
            copies.append(pltpu.make_async_copy(update.at[at, :], out_ref.at[at, :], sems.at[len(copies)]))
            copies[-1].start()
    for copy in copies:
        copy.wait()


def per_device(sim_lai, owner_ids, cloud_words, scene_lai, scene_sigma, mtf_taps):
    n_tile, n_mem = lax.axis_size("tile"), lax.axis_size("member")
    _, tiles, members, rows, cols = sim_lai.shape
    half_r, half_c = rows // 2, cols // 2
    chunk = chunk_tiles(tiles, members, rows)
    sizes = (tiles, chunk, members, rows, cols)
    fields = chunk * members
    fr, fh = fields * rows, fields * half_r
    cuts = PIECES if fields % PIECES == 0 else 1
    vmem = pl.BlockSpec(memory_space=pltpu.VMEM)
    smem = pl.BlockSpec(memory_space=pltpu.SMEM)
    here = lambda x: pltpu.with_memory_space_constraint(x, pltpu.VMEM)
    scalars = lambda x: pltpu.with_memory_space_constraint(x, pltpu.SMEM)
    steps = plan(n_tile, n_mem)
    block = pltpu.VMEM((2, CAP, half_r, half_c), jnp.bfloat16)
    *blocks, own = pl.pallas_call(
        lambda *refs: pack(steps, (n_tile, n_mem), *refs),
        out_shape=[block] * (n_tile + 1),
        in_specs=[vmem] * 2,
        out_specs=[vmem] * (n_tile + 1),
        name="pack",
    )(scene_lai[0, 0], scene_sigma[0, 0])
    n_date = lax.axis_size("date")
    arrived = [here(lax.ppermute(blocks[p], GROUP, pairs(steps[p], n_date))) for p in range(n_tile)]
    pred, valid, colt, rowt, picks = pl.pallas_call(
        lambda *refs: before(sizes, (n_tile, n_mem), *refs),
        out_shape=(
            pltpu.VMEM((tiles * members * half_r, half_c), jnp.bfloat16),
            pltpu.VMEM((tiles * half_r, half_c), jnp.float32),
            pltpu.VMEM((half_c, cols), jnp.bfloat16),
            pltpu.VMEM((fr // cuts, fh // cuts), jnp.bfloat16),
            pltpu.SMEM((tiles,), jnp.int32),
        ),
        in_specs=[smem, vmem, vmem, pl.BlockSpec(memory_space=pl.ANY)],
        out_specs=[vmem] * 4 + [smem],
        scratch_shapes=[
            pltpu.VMEM((tiles, 128), jnp.int32),
            pltpu.VMEM((cols, half_c), jnp.bfloat16),
            pltpu.VMEM((fh, fr), jnp.bfloat16),
            pltpu.VMEM((tiles * members * rows, cols), jnp.bfloat16),
            pltpu.SemaphoreType.DMA,
        ],
        name="before",
    )(owner_ids, mtf_taps, cloud_words[0], sim_lai.reshape(tiles * members * rows, cols))
    out = pl.pallas_call(
        lambda *refs: after(sizes, n_tile, *refs),
        out_shape=jax.ShapeDtypeStruct((tiles * members * rows, cols), jnp.bfloat16),
        in_specs=[smem] + [vmem] * (5 + n_tile),
        out_specs=pl.BlockSpec(memory_space=pl.ANY),
        scratch_shapes=[
            pltpu.VMEM(((n_tile + 1) * CAP, 2, half_r, half_c), jnp.bfloat16),
            pltpu.VMEM((tiles * members * rows, cols), jnp.bfloat16),
            pltpu.SemaphoreType.DMA((cuts * tiles // chunk,)),
        ],
        name="after",
    )(scalars(picks), *[here(x) for x in (pred, valid, colt, rowt, own)], *arrived)
    return out.reshape(sim_lai.shape)


def solution(mesh):
    placed = (
        P("date", ("region", "tile"), "member", None, None),
        P("date", ("region", "tile")),
        P("date", ("region", "tile"), None),
        P("date", ("region", "tile"), "member", None, None),
        P("date", ("region", "tile"), "member", None, None),
        P(),
    )
    return jax.shard_map(
        per_device,
        mesh=mesh,
        in_specs=placed,
        out_specs=P("date", ("region", "tile"), "member", None, None),
        check_vma=False,
    )
```

```python
import jax
import jax.numpy as jnp
from jax import lax
from jax.experimental import pallas as pl
from jax.experimental.pallas import tpu as pltpu
from jax.sharding import PartitionSpec as P

CAP = 2
PIECES = 2
GROUP = ("tile", "member", "date")


TUNED = {
    (4, 2): (
        (3, 4, 2, 6, 1, 5, 0, 7),
        (1, 5, 3, 7, 0, 4, 2, 6),
        (2, 6, 0, 5, 3, 7, 1, 4),
        (0, 7, 1, 4, 2, 6, 3, 5),
    ),
}


def plan(n_tile, n_mem):
    if (n_tile, n_mem) in TUNED:
        return TUNED[n_tile, n_mem]
    per = n_tile // n_mem
    steps = []
    for k in range(per):
        for j in range(n_mem):
            to = [
                (mm * per + (o + k) % per) * n_mem + (o // per + j) % n_mem
                for o in range(n_tile)
                for mm in range(n_mem)
            ]
            steps.append(tuple(to))
    return tuple(steps)


def pairs(to, n_date):
    return [
        (src * n_date + d, dst * n_date + (d if src != dst else (d + 1) % n_date))
        for src, dst in enumerate(to)
        for d in range(n_date)
    ]


def packed(values, width, index):
    word = sum(v << (width * i) for i, v in enumerate(values))
    return jnp.bitwise_and(jnp.right_shift(jnp.int32(word), index * width), (1 << width) - 1)


def sent_block(n_tile, n_mem, step, to):
    per = n_tile // n_mem
    here, member = lax.axis_index("tile"), lax.axis_index("member")
    if (n_tile, n_mem) not in TUNED:
        return (here + step // n_mem) % per
    width = max(1, (per - 1).bit_length())
    sources = [t // n_mem % per for t in to]
    return packed(sources, width, here * n_mem + member)


def arrival(n_tile, n_mem, owner):
    per = n_tile // n_mem
    here, member = lax.axis_index("tile"), lax.axis_index("member")
    if (n_tile, n_mem) in TUNED:
        device = here * n_mem + member
        steps = TUNED[n_tile, n_mem]
        width = n_tile.bit_length()
        out = jnp.int32(0)
        for o in range(n_tile):
            came = []
            for d in range(n_tile * n_mem):
                holder = o * n_mem + d // n_mem // per
                came.append(n_tile if holder == d else [to[holder] for to in steps].index(d))
            out = jnp.where(owner == o, packed(came, width, device), out)
        return out
    k, j = (here - owner) % per, (member - owner // per) % n_mem
    mine = jnp.logical_and(owner == here, here // per == member)
    return jnp.where(mine, n_tile, k * n_mem + j)


def chunk_tiles(tiles, members, rows):
    best = 1
    for c in range(1, tiles + 1):
        if tiles % c == 0 and c * members * rows <= 256:
            best = c
    return best


def iota(shape, dim):
    return lax.broadcasted_iota(jnp.int32, shape, dim)


def pack(steps, ring, owners_ref, scene_ref, sigma_ref, taps_ref, words_ref, *outs):
    n_tile, n_mem = ring
    per = n_tile // n_mem
    blocks, (own_ref, taps_out, words_out, owners_out) = outs[:n_tile], outs[n_tile:]
    for p in range(n_tile):
        at = pl.ds(sent_block(n_tile, n_mem, p, steps[p]) * CAP, CAP)
        blocks[p][0] = scene_ref[at]
        blocks[p][1] = sigma_ref[at]
    at = pl.ds(lax.axis_index("tile") % per * CAP, CAP)
    own_ref[0] = scene_ref[at]
    own_ref[1] = sigma_ref[at]
    taps_out[...] = taps_ref[...]
    words_out[...] = words_ref[...]
    for t in range(owners_ref.shape[1]):
        owners_out[t] = owners_ref[0, t]


class Band:
    def __init__(self, taps, shape):
        self.taps = [jnp.broadcast_to(tap, shape) for tap in taps]
        self.shape, self.made = shape, {}
        self.row, self.lane = iota(shape, 0), iota(shape, 1)

    def tile(self, row_mul, lane_mul, offset, first=None, length=None):
        ends = [offset + r * row_mul * (self.shape[0] - 1) + c * lane_mul * (self.shape[1] - 1) for r in (0, 1) for c in (0, 1)]
        outside = max(ends) < 0 or min(ends) >= len(self.taps)
        if first is not None:
            outside = outside or first >= self.shape[1] or first + length <= 0
        key = None if outside else (row_mul, lane_mul, offset, first)
        if key not in self.made:
            out = jnp.zeros(self.shape, jnp.float32)
            if not outside:
                which = self.row * row_mul + self.lane * lane_mul + offset
                if first is not None:
                    inside = jnp.logical_and(self.lane >= first, self.lane < first + length)
                    which = jnp.where(inside, which, -1)
                for k, tap in enumerate(self.taps):
                    out = jnp.where(which == k, tap, out)
            self.made[key] = out.astype(jnp.bfloat16)
        return self.made[key]


def before(sizes, ring, owners_ref, taps_ref, words_ref, lai_ref, pred_ref, valid_ref, colt_ref, rowt_ref, pick_ref, *scratch):
    tiles, chunk, members, rows, cols = sizes
    half_r, half_c = rows // 2, cols // 2
    n_words = words_ref.shape[1]
    pad, col, rowd, field_ref, sem = scratch
    fetch = pltpu.make_async_copy(lai_ref, field_ref, sem)
    fetch.start()
    owner = [owners_ref[t] for t in range(tiles)]
    for t in range(tiles):
        rank = 0
        for u in range(t):
            rank = rank + jnp.where(owner[u] == owner[t], 1, 0)
        pick_ref[t] = arrival(*ring, owner[t]) * CAP + rank
    taps = taps_ref[...]
    taps = taps / jnp.sum(taps, axis=1, keepdims=True)
    reach = taps.shape[1] // 2
    fields = chunk * members
    fr, fh = fields * rows, fields * half_r
    high, wide = 16, 128
    down = Band([taps[0:1, k : k + 1] for k in range(taps.shape[1])], (high, wide))
    across = Band([taps[1:2, k : k + 1] for k in range(taps.shape[1])], (high, wide))
    for r in range(0, cols, high):
        for c in range(0, half_c, wide):
            col[r : r + high, c : c + wide] = across.tile(1, -2, r - 2 * c + reach)
    for r in range(0, half_c, high):
        for c in range(0, cols, wide):
            colt_ref[r : r + high, c : c + wide] = across.tile(-2, 1, c - 2 * r + reach)
    for r in range(0, fh, high):
        top = r // half_r * rows
        for c in range(0, fr, wide):
            rowd[r : r + high, c : c + wide] = down.tile(-2, 1, c - top - 2 * (r % half_r) + reach, top - c, rows)
    for r in range(0, rowt_ref.shape[0], high):
        left = r // rows * half_r
        width = min(wide, rowt_ref.shape[1])
        for c in range(0, rowt_ref.shape[1], width):
            tile = down.tile(1, -2, r % rows + 2 * (left - c) + reach, left - c, half_r)
            rowt_ref[r : r + high, c : c + width] = tile[:, :width]
    pad[...] = jnp.zeros(pad.shape, jnp.int32)
    pad[:, :n_words] = words_ref[...]
    per_row = half_c // 2 // 32
    for i0 in range(0, half_r, 8):
        for j0 in range(0, half_c, wide):
            i = iota((8, wide), 0) + i0
            j = iota((8, wide), 1) + j0
            which = jnp.right_shift(i, 1) * per_row + jnp.right_shift(j, 6)
            shift = jnp.bitwise_and(jnp.right_shift(j, 1), 31)
            for t in range(tiles):
                words = jnp.broadcast_to(pad[t : t + 1, :], (8, wide))
                word = jnp.take_along_axis(words, which, axis=1)
                bit = jnp.bitwise_and(jnp.right_shift(word, shift), 1)
                valid_ref[t * half_r + i0 : t * half_r + i0 + 8, j0 : j0 + wide] = bit.astype(jnp.float32)
    fetch.wait()
    for g in range(tiles // chunk):
        field = field_ref[g * fr : (g + 1) * fr, :]
        blurred = jnp.dot(rowd[...], field, preferred_element_type=jnp.float32).astype(jnp.bfloat16)
        pred_ref[g * fh : (g + 1) * fh, :] = jnp.dot(
            blurred, col[...], preferred_element_type=jnp.float32
        ).astype(jnp.bfloat16)


def after(sizes, n_tile, pick_ref, pred_ref, valid_ref, colt_ref, rowt_ref, own_ref, *refs):
    tiles, chunk, members, rows, cols = sizes
    half_r, half_c = rows // 2, cols // 2
    arrived, out_ref, scenes, update, sems = refs[:n_tile], refs[n_tile], *refs[n_tile + 1 :]
    fields = chunk * members
    fr, fh = fields * rows, fields * half_r
    for p, block in enumerate((*arrived, own_ref)):
        for r in range(CAP):
            for kind in range(2):
                scenes[p * CAP + r, kind] = block[kind, r]
    pr, ph = rowt_ref.shape
    cuts = fr // pr
    copies = []
    for g in range(tiles // chunk):
        parts = []
        for t in range(g * chunk, (g + 1) * chunk):
            seen = scenes[pick_ref[t], 0].astype(jnp.float32)
            sigma = scenes[pick_ref[t], 1].astype(jnp.float32)
            weight = valid_ref[t * half_r : (t + 1) * half_r, :] / (sigma * sigma)
            for m in range(members):
                at = (t * members + m) * half_r
                gap = seen - pred_ref[at : at + half_r, :].astype(jnp.float32)
                parts.append((gap * weight).astype(jnp.bfloat16))
        misfit = jnp.concatenate(parts, axis=0)
        spread = jnp.dot(misfit, colt_ref[...], preferred_element_type=jnp.float32).astype(jnp.bfloat16)
        for c in range(cuts):
            at = pl.ds(g * fr + c * pr, pr)
            update[at, :] = jnp.dot(
                rowt_ref[...], spread[c * ph : (c + 1) * ph, :], preferred_element_type=jnp.float32
            ).astype(jnp.bfloat16)
            copies.append(pltpu.make_async_copy(update.at[at, :], out_ref.at[at, :], sems.at[len(copies)]))
            copies[-1].start()
    for copy in copies:
        copy.wait()


def per_device(sim_lai, owner_ids, cloud_words, scene_lai, scene_sigma, mtf_taps):
    n_tile, n_mem = lax.axis_size("tile"), lax.axis_size("member")
    _, tiles, members, rows, cols = sim_lai.shape
    half_r, half_c = rows // 2, cols // 2
    chunk = chunk_tiles(tiles, members, rows)
    sizes = (tiles, chunk, members, rows, cols)
    fields = chunk * members
    fr, fh = fields * rows, fields * half_r
    cuts = PIECES if fields % PIECES == 0 else 1
    vmem = pl.BlockSpec(memory_space=pltpu.VMEM)
    smem = pl.BlockSpec(memory_space=pltpu.SMEM)
    here = lambda x: pltpu.with_memory_space_constraint(x, pltpu.VMEM)
    scalars = lambda x: pltpu.with_memory_space_constraint(x, pltpu.SMEM)
    steps = plan(n_tile, n_mem)
    block = pltpu.VMEM((2, CAP, half_r, half_c), jnp.bfloat16)
    *blocks, own, taps, words, owners = pl.pallas_call(
        lambda *refs: pack(steps, (n_tile, n_mem), *refs),
        out_shape=(
            *[block] * (n_tile + 1),
            pltpu.VMEM(mtf_taps.shape, jnp.float32),
            pltpu.VMEM(cloud_words.shape[1:], jnp.int32),
            pltpu.SMEM((tiles,), jnp.int32),
        ),
        in_specs=[smem] + [vmem] * 4,
        out_specs=[vmem] * (n_tile + 3) + [smem],
        name="pack",
    )(owner_ids, scene_lai[0, 0], scene_sigma[0, 0], mtf_taps, cloud_words[0])
    n_date = lax.axis_size("date")
    arrived = [here(lax.ppermute(blocks[p], GROUP, pairs(steps[p], n_date))) for p in range(n_tile)]
    pred, valid, colt, rowt, picks = pl.pallas_call(
        lambda *refs: before(sizes, (n_tile, n_mem), *refs),
        out_shape=(
            pltpu.VMEM((tiles * members * half_r, half_c), jnp.bfloat16),
            pltpu.VMEM((tiles * half_r, half_c), jnp.float32),
            pltpu.VMEM((half_c, cols), jnp.bfloat16),
            pltpu.VMEM((fr // cuts, fh // cuts), jnp.bfloat16),
            pltpu.SMEM((tiles,), jnp.int32),
        ),
        in_specs=[smem, vmem, vmem, pl.BlockSpec(memory_space=pl.ANY)],
        out_specs=[vmem] * 4 + [smem],
        scratch_shapes=[
            pltpu.VMEM((tiles, 128), jnp.int32),
            pltpu.VMEM((cols, half_c), jnp.bfloat16),
            pltpu.VMEM((fh, fr), jnp.bfloat16),
            pltpu.VMEM((tiles * members * rows, cols), jnp.bfloat16),
            pltpu.SemaphoreType.DMA,
        ],
        name="before",
    )(scalars(owners), here(taps), here(words), sim_lai.reshape(tiles * members * rows, cols))
    out = pl.pallas_call(
        lambda *refs: after(sizes, n_tile, *refs),
        out_shape=jax.ShapeDtypeStruct((tiles * members * rows, cols), jnp.bfloat16),
        in_specs=[smem] + [vmem] * (5 + n_tile),
        out_specs=pl.BlockSpec(memory_space=pl.ANY),
        scratch_shapes=[
            pltpu.VMEM(((n_tile + 1) * CAP, 2, half_r, half_c), jnp.bfloat16),
            pltpu.VMEM((tiles * members * rows, cols), jnp.bfloat16),
            pltpu.SemaphoreType.DMA((cuts * tiles // chunk,)),
        ],
        name="after",
    )(scalars(picks), *[here(x) for x in (pred, valid, colt, rowt, own)], *arrived)
    return out.reshape(sim_lai.shape)


def solution(mesh):
    placed = (
        P("date", ("region", "tile"), "member", None, None),
        P("date", ("region", "tile")),
        P("date", ("region", "tile"), None),
        P("date", ("region", "tile"), "member", None, None),
        P("date", ("region", "tile"), "member", None, None),
        P(),
    )
    return jax.shard_map(
        per_device,
        mesh=mesh,
        in_specs=placed,
        out_specs=P("date", ("region", "tile"), "member", None, None),
        check_vma=False,
    )
```

```python
import jax
import jax.numpy as jnp
from jax import lax
from jax.experimental import pallas as pl
from jax.experimental.pallas import tpu as pltpu
from jax.sharding import PartitionSpec as P

CAP = 2
PIECES = 4
GROUP = ("tile", "member", "date")


TUNED = {
    (4, 2): (
        (3, 4, 2, 6, 1, 5, 0, 7),
        (1, 5, 3, 7, 0, 4, 2, 6),
        (2, 6, 0, 5, 3, 7, 1, 4),
        (0, 7, 1, 4, 2, 6, 3, 5),
    ),
}


def plan(n_tile, n_mem):
    if (n_tile, n_mem) in TUNED:
        return TUNED[n_tile, n_mem]
    per = n_tile // n_mem
    steps = []
    for k in range(per):
        for j in range(n_mem):
            to = [
                (mm * per + (o + k) % per) * n_mem + (o // per + j) % n_mem
                for o in range(n_tile)
                for mm in range(n_mem)
            ]
            steps.append(tuple(to))
    return tuple(steps)


def pairs(to, n_date):
    return [
        (src * n_date + d, dst * n_date + (d if src != dst else (d + 1) % n_date))
        for src, dst in enumerate(to)
        for d in range(n_date)
    ]


def packed(values, width, index):
    word = sum(v << (width * i) for i, v in enumerate(values))
    return jnp.bitwise_and(jnp.right_shift(jnp.int32(word), index * width), (1 << width) - 1)


def sent_block(n_tile, n_mem, step, to):
    per = n_tile // n_mem
    here, member = lax.axis_index("tile"), lax.axis_index("member")
    if (n_tile, n_mem) not in TUNED:
        return (here + step // n_mem) % per
    width = max(1, (per - 1).bit_length())
    sources = [t // n_mem % per for t in to]
    return packed(sources, width, here * n_mem + member)


def arrival(n_tile, n_mem, owner):
    per = n_tile // n_mem
    here, member = lax.axis_index("tile"), lax.axis_index("member")
    if (n_tile, n_mem) in TUNED:
        device = here * n_mem + member
        steps = TUNED[n_tile, n_mem]
        width = n_tile.bit_length()
        out = jnp.int32(0)
        for o in range(n_tile):
            came = []
            for d in range(n_tile * n_mem):
                holder = o * n_mem + d // n_mem // per
                came.append(n_tile if holder == d else [to[holder] for to in steps].index(d))
            out = jnp.where(owner == o, packed(came, width, device), out)
        return out
    k, j = (here - owner) % per, (member - owner // per) % n_mem
    mine = jnp.logical_and(owner == here, here // per == member)
    return jnp.where(mine, n_tile, k * n_mem + j)


def chunk_tiles(tiles, members, rows):
    best = 1
    for c in range(1, tiles + 1):
        if tiles % c == 0 and c * members * rows <= 256:
            best = c
    return best


def iota(shape, dim):
    return lax.broadcasted_iota(jnp.int32, shape, dim)


def pack(steps, ring, scene_ref, sigma_ref, *outs):
    n_tile, n_mem = ring
    per = n_tile // n_mem
    blocks, (own_ref,) = outs[:n_tile], outs[n_tile:]
    for p in range(n_tile):
        at = pl.ds(sent_block(n_tile, n_mem, p, steps[p]) * CAP, CAP)
        blocks[p][0] = scene_ref[at]
        blocks[p][1] = sigma_ref[at]
    at = pl.ds(lax.axis_index("tile") % per * CAP, CAP)
    own_ref[0] = scene_ref[at]
    own_ref[1] = sigma_ref[at]


class Band:
    def __init__(self, taps, shape):
        self.taps = [jnp.broadcast_to(tap, shape) for tap in taps]
        self.shape, self.made = shape, {}
        self.row, self.lane = iota(shape, 0), iota(shape, 1)

    def tile(self, row_mul, lane_mul, offset, first=None, length=None):
        ends = [offset + r * row_mul * (self.shape[0] - 1) + c * lane_mul * (self.shape[1] - 1) for r in (0, 1) for c in (0, 1)]
        outside = max(ends) < 0 or min(ends) >= len(self.taps)
        if first is not None:
            outside = outside or first >= self.shape[1] or first + length <= 0
        key = None if outside else (row_mul, lane_mul, offset, first)
        if key not in self.made:
            out = jnp.zeros(self.shape, jnp.float32)
            if not outside:
                which = self.row * row_mul + self.lane * lane_mul + offset
                if first is not None:
                    inside = jnp.logical_and(self.lane >= first, self.lane < first + length)
                    which = jnp.where(inside, which, -1)
                for k, tap in enumerate(self.taps):
                    out = jnp.where(which == k, tap, out)
            self.made[key] = out.astype(jnp.bfloat16)
        return self.made[key]


def before(sizes, ring, owners_ref, taps_ref, words_ref, lai_ref, pred_ref, valid_ref, colt_ref, rowt_ref, pick_ref, *scratch):
    tiles, chunk, members, rows, cols = sizes
    half_r, half_c = rows // 2, cols // 2
    n_words = words_ref.shape[1]
    pad, col, rowd, field_ref, sem = scratch
    fetch = pltpu.make_async_copy(lai_ref, field_ref, sem)
    fetch.start()
    owner = [owners_ref[0, t] for t in range(tiles)]
    for t in range(tiles):
        rank = 0
        for u in range(t):
            rank = rank + jnp.where(owner[u] == owner[t], 1, 0)
        pick_ref[t] = arrival(*ring, owner[t]) * CAP + rank
    taps = taps_ref[...]
    taps = taps / jnp.sum(taps, axis=1, keepdims=True)
    reach = taps.shape[1] // 2
    fields = chunk * members
    fr, fh = fields * rows, fields * half_r
    high, wide = 16, 128
    down = Band([taps[0:1, k : k + 1] for k in range(taps.shape[1])], (high, wide))
    across = Band([taps[1:2, k : k + 1] for k in range(taps.shape[1])], (high, wide))
    for r in range(0, cols, high):
        for c in range(0, half_c, wide):
            col[r : r + high, c : c + wide] = across.tile(1, -2, r - 2 * c + reach)
    for r in range(0, half_c, high):
        for c in range(0, cols, wide):
            colt_ref[r : r + high, c : c + wide] = across.tile(-2, 1, c - 2 * r + reach)
    for r in range(0, fh, high):
        top = r // half_r * rows
        for c in range(0, fr, wide):
            rowd[r : r + high, c : c + wide] = down.tile(-2, 1, c - top - 2 * (r % half_r) + reach, top - c, rows)
    for r in range(0, rowt_ref.shape[0], high):
        left = r // rows * half_r
        width = min(wide, rowt_ref.shape[1])
        for c in range(0, rowt_ref.shape[1], width):
            tile = down.tile(1, -2, r % rows + 2 * (left - c) + reach, left - c, half_r)
            rowt_ref[r : r + high, c : c + width] = tile[:, :width]
    pad[...] = jnp.zeros(pad.shape, jnp.int32)
    pad[:, :n_words] = words_ref[...]
    per_row = half_c // 2 // 32
    for i0 in range(0, half_r, 8):
        for j0 in range(0, half_c, wide):
            i = iota((8, wide), 0) + i0
            j = iota((8, wide), 1) + j0
            which = jnp.right_shift(i, 1) * per_row + jnp.right_shift(j, 6)
            shift = jnp.bitwise_and(jnp.right_shift(j, 1), 31)
            for t in range(tiles):
                words = jnp.broadcast_to(pad[t : t + 1, :], (8, wide))
                word = jnp.take_along_axis(words, which, axis=1)
                bit = jnp.bitwise_and(jnp.right_shift(word, shift), 1)
                valid_ref[t * half_r + i0 : t * half_r + i0 + 8, j0 : j0 + wide] = bit.astype(jnp.float32)
    fetch.wait()
    for g in range(tiles // chunk):
        field = field_ref[g * fr : (g + 1) * fr, :]
        blurred = jnp.dot(rowd[...], field, preferred_element_type=jnp.float32).astype(jnp.bfloat16)
        pred_ref[g * fh : (g + 1) * fh, :] = jnp.dot(
            blurred, col[...], preferred_element_type=jnp.float32
        ).astype(jnp.bfloat16)


def after(sizes, n_tile, pick_ref, pred_ref, valid_ref, colt_ref, rowt_ref, own_ref, *refs):
    tiles, chunk, members, rows, cols = sizes
    half_r, half_c = rows // 2, cols // 2
    arrived, out_ref, scenes, update, sems = refs[:n_tile], refs[n_tile], *refs[n_tile + 1 :]
    fields = chunk * members
    fr, fh = fields * rows, fields * half_r
    for p, block in enumerate((*arrived, own_ref)):
        for r in range(CAP):
            for kind in range(2):
                scenes[p * CAP + r, kind] = block[kind, r]
    pr, ph = rowt_ref.shape
    cuts = fr // pr
    copies = []
    for g in range(tiles // chunk):
        parts = []
        for t in range(g * chunk, (g + 1) * chunk):
            seen = scenes[pick_ref[t], 0].astype(jnp.float32)
            sigma = scenes[pick_ref[t], 1].astype(jnp.float32)
            weight = valid_ref[t * half_r : (t + 1) * half_r, :] / (sigma * sigma)
            for m in range(members):
                at = (t * members + m) * half_r
                gap = seen - pred_ref[at : at + half_r, :].astype(jnp.float32)
                parts.append((gap * weight).astype(jnp.bfloat16))
        misfit = jnp.concatenate(parts, axis=0)
        spread = jnp.dot(misfit, colt_ref[...], preferred_element_type=jnp.float32).astype(jnp.bfloat16)
        for c in range(cuts):
            at = pl.ds(g * fr + c * pr, pr)
            update[at, :] = jnp.dot(
                rowt_ref[...], spread[c * ph : (c + 1) * ph, :], preferred_element_type=jnp.float32
            ).astype(jnp.bfloat16)
            copies.append(pltpu.make_async_copy(update.at[at, :], out_ref.at[at, :], sems.at[len(copies)]))
            copies[-1].start()
    for copy in copies:
        copy.wait()


def per_device(sim_lai, owner_ids, cloud_words, scene_lai, scene_sigma, mtf_taps):
    n_tile, n_mem = lax.axis_size("tile"), lax.axis_size("member")
    _, tiles, members, rows, cols = sim_lai.shape
    half_r, half_c = rows // 2, cols // 2
    chunk = chunk_tiles(tiles, members, rows)
    sizes = (tiles, chunk, members, rows, cols)
    fields = chunk * members
    fr, fh = fields * rows, fields * half_r
    cuts = PIECES if fields % PIECES == 0 else 1
    vmem = pl.BlockSpec(memory_space=pltpu.VMEM)
    smem = pl.BlockSpec(memory_space=pltpu.SMEM)
    here = lambda x: pltpu.with_memory_space_constraint(x, pltpu.VMEM)
    scalars = lambda x: pltpu.with_memory_space_constraint(x, pltpu.SMEM)
    steps = plan(n_tile, n_mem)
    block = pltpu.VMEM((2, CAP, half_r, half_c), jnp.bfloat16)
    *blocks, own = pl.pallas_call(
        lambda *refs: pack(steps, (n_tile, n_mem), *refs),
        out_shape=[block] * (n_tile + 1),
        in_specs=[vmem] * 2,
        out_specs=[vmem] * (n_tile + 1),
        name="pack",
    )(scene_lai[0, 0], scene_sigma[0, 0])
    n_date = lax.axis_size("date")
    arrived = [here(lax.ppermute(blocks[p], GROUP, pairs(steps[p], n_date))) for p in range(n_tile)]
    pred, valid, colt, rowt, picks = pl.pallas_call(
        lambda *refs: before(sizes, (n_tile, n_mem), *refs),
        out_shape=(
            pltpu.VMEM((tiles * members * half_r, half_c), jnp.bfloat16),
            pltpu.VMEM((tiles * half_r, half_c), jnp.float32),
            pltpu.VMEM((half_c, cols), jnp.bfloat16),
            pltpu.VMEM((fr // cuts, fh // cuts), jnp.bfloat16),
            pltpu.SMEM((tiles,), jnp.int32),
        ),
        in_specs=[smem, vmem, vmem, pl.BlockSpec(memory_space=pl.ANY)],
        out_specs=[vmem] * 4 + [smem],
        scratch_shapes=[
            pltpu.VMEM((tiles, 128), jnp.int32),
            pltpu.VMEM((cols, half_c), jnp.bfloat16),
            pltpu.VMEM((fh, fr), jnp.bfloat16),
            pltpu.VMEM((tiles * members * rows, cols), jnp.bfloat16),
            pltpu.SemaphoreType.DMA,
        ],
        name="before",
    )(owner_ids, mtf_taps, cloud_words[0], sim_lai.reshape(tiles * members * rows, cols))
    out = pl.pallas_call(
        lambda *refs: after(sizes, n_tile, *refs),
        out_shape=jax.ShapeDtypeStruct((tiles * members * rows, cols), jnp.bfloat16),
        in_specs=[smem] + [vmem] * (5 + n_tile),
        out_specs=pl.BlockSpec(memory_space=pl.ANY),
        scratch_shapes=[
            pltpu.VMEM(((n_tile + 1) * CAP, 2, half_r, half_c), jnp.bfloat16),
            pltpu.VMEM((tiles * members * rows, cols), jnp.bfloat16),
            pltpu.SemaphoreType.DMA((cuts * tiles // chunk,)),
        ],
        name="after",
    )(scalars(picks), *[here(x) for x in (pred, valid, colt, rowt, own)], *arrived)
    return out.reshape(sim_lai.shape)


def solution(mesh):
    placed = (
        P("date", ("region", "tile"), "member", None, None),
        P("date", ("region", "tile")),
        P("date", ("region", "tile"), None),
        P("date", ("region", "tile"), "member", None, None),
        P("date", ("region", "tile"), "member", None, None),
        P(),
    )
    return jax.shard_map(
        per_device,
        mesh=mesh,
        in_specs=placed,
        out_specs=P("date", ("region", "tile"), "member", None, None),
        check_vma=False,
    )
```

```python
import jax
import jax.numpy as jnp
from jax import lax
from jax.experimental import pallas as pl
from jax.experimental.pallas import tpu as pltpu
from jax.sharding import PartitionSpec as P

CAP = 2
PIECES = 4
GROUP = ("tile", "member", "date")


TUNED = {
    (4, 2): (
        (3, 4, 2, 6, 1, 5, 0, 7),
        (1, 5, 3, 7, 0, 4, 2, 6),
        (2, 6, 0, 5, 3, 7, 1, 4),
        (0, 7, 1, 4, 2, 6, 3, 5),
    ),
}


def plan(n_tile, n_mem):
    if (n_tile, n_mem) in TUNED:
        return TUNED[n_tile, n_mem]
    per = n_tile // n_mem
    steps = []
    for k in range(per):
        for j in range(n_mem):
            to = [
                (mm * per + (o + k) % per) * n_mem + (o // per + j) % n_mem
                for o in range(n_tile)
                for mm in range(n_mem)
            ]
            steps.append(tuple(to))
    return tuple(steps)


def pairs(to, n_date):
    return [
        (src * n_date + d, dst * n_date + (d if src != dst else (d + 1) % n_date))
        for src, dst in enumerate(to)
        for d in range(n_date)
    ]


def packed(values, width, index):
    word = sum(v << (width * i) for i, v in enumerate(values))
    return jnp.bitwise_and(jnp.right_shift(jnp.int32(word), index * width), (1 << width) - 1)


def sent_block(n_tile, n_mem, step, to):
    per = n_tile // n_mem
    here, member = lax.axis_index("tile"), lax.axis_index("member")
    if (n_tile, n_mem) not in TUNED:
        return (here + step // n_mem) % per
    width = max(1, (per - 1).bit_length())
    sources = [t // n_mem % per for t in to]
    return packed(sources, width, here * n_mem + member)


def arrival(n_tile, n_mem, owner):
    per = n_tile // n_mem
    here, member = lax.axis_index("tile"), lax.axis_index("member")
    if (n_tile, n_mem) in TUNED:
        device = here * n_mem + member
        steps = TUNED[n_tile, n_mem]
        width = n_tile.bit_length()
        out = jnp.int32(0)
        for o in range(n_tile):
            came = []
            for d in range(n_tile * n_mem):
                holder = o * n_mem + d // n_mem // per
                came.append(n_tile if holder == d else [to[holder] for to in steps].index(d))
            out = jnp.where(owner == o, packed(came, width, device), out)
        return out
    k, j = (here - owner) % per, (member - owner // per) % n_mem
    mine = jnp.logical_and(owner == here, here // per == member)
    return jnp.where(mine, n_tile, k * n_mem + j)


def chunk_tiles(tiles, members, rows):
    best = 1
    for c in range(1, tiles + 1):
        if tiles % c == 0 and c * members * rows <= 256:
            best = c
    return best


def iota(shape, dim):
    return lax.broadcasted_iota(jnp.int32, shape, dim)


def pack(steps, ring, owners_ref, scene_ref, sigma_ref, taps_ref, words_ref, *outs):
    n_tile, n_mem = ring
    per = n_tile // n_mem
    blocks, (own_ref, taps_out, words_out, owners_out) = outs[:n_tile], outs[n_tile:]
    for p in range(n_tile):
        at = pl.ds(sent_block(n_tile, n_mem, p, steps[p]) * CAP, CAP)
        blocks[p][0] = scene_ref[at]
        blocks[p][1] = sigma_ref[at]
    at = pl.ds(lax.axis_index("tile") % per * CAP, CAP)
    own_ref[0] = scene_ref[at]
    own_ref[1] = sigma_ref[at]
    taps_out[...] = taps_ref[...]
    words_out[...] = words_ref[...]
    for t in range(owners_ref.shape[1]):
        owners_out[t] = owners_ref[0, t]


class Band:
    def __init__(self, taps, shape):
        self.taps = [jnp.broadcast_to(tap, shape) for tap in taps]
        self.shape, self.made = shape, {}
        self.row, self.lane = iota(shape, 0), iota(shape, 1)

    def tile(self, row_mul, lane_mul, offset, first=None, length=None):
        ends = [offset + r * row_mul * (self.shape[0] - 1) + c * lane_mul * (self.shape[1] - 1) for r in (0, 1) for c in (0, 1)]
        outside = max(ends) < 0 or min(ends) >= len(self.taps)
        if first is not None:
            outside = outside or first >= self.shape[1] or first + length <= 0
        key = None if outside else (row_mul, lane_mul, offset, first)
        if key not in self.made:
            out = jnp.zeros(self.shape, jnp.float32)
            if not outside:
                which = self.row * row_mul + self.lane * lane_mul + offset
                if first is not None:
                    inside = jnp.logical_and(self.lane >= first, self.lane < first + length)
                    which = jnp.where(inside, which, -1)
                for k, tap in enumerate(self.taps):
                    out = jnp.where(which == k, tap, out)
            self.made[key] = out.astype(jnp.bfloat16)
        return self.made[key]


def before(sizes, ring, owners_ref, taps_ref, words_ref, lai_ref, pred_ref, valid_ref, colt_ref, rowt_ref, pick_ref, *scratch):
    tiles, chunk, members, rows, cols = sizes
    half_r, half_c = rows // 2, cols // 2
    n_words = words_ref.shape[1]
    pad, col, rowd, field_ref, sem = scratch
    fetch = pltpu.make_async_copy(lai_ref, field_ref, sem)
    fetch.start()
    owner = [owners_ref[t] for t in range(tiles)]
    for t in range(tiles):
        rank = 0
        for u in range(t):
            rank = rank + jnp.where(owner[u] == owner[t], 1, 0)
        pick_ref[t] = arrival(*ring, owner[t]) * CAP + rank
    taps = taps_ref[...]
    taps = taps / jnp.sum(taps, axis=1, keepdims=True)
    reach = taps.shape[1] // 2
    fields = chunk * members
    fr, fh = fields * rows, fields * half_r
    high, wide = 16, 128
    down = Band([taps[0:1, k : k + 1] for k in range(taps.shape[1])], (high, wide))
    across = Band([taps[1:2, k : k + 1] for k in range(taps.shape[1])], (high, wide))
    for r in range(0, cols, high):
        for c in range(0, half_c, wide):
            col[r : r + high, c : c + wide] = across.tile(1, -2, r - 2 * c + reach)
    for r in range(0, half_c, high):
        for c in range(0, cols, wide):
            colt_ref[r : r + high, c : c + wide] = across.tile(-2, 1, c - 2 * r + reach)
    for r in range(0, fh, high):
        top = r // half_r * rows
        for c in range(0, fr, wide):
            rowd[r : r + high, c : c + wide] = down.tile(-2, 1, c - top - 2 * (r % half_r) + reach, top - c, rows)
    for r in range(0, rowt_ref.shape[0], high):
        left = r // rows * half_r
        width = min(wide, rowt_ref.shape[1])
        for c in range(0, rowt_ref.shape[1], width):
            tile = down.tile(1, -2, r % rows + 2 * (left - c) + reach, left - c, half_r)
            rowt_ref[r : r + high, c : c + width] = tile[:, :width]
    pad[...] = jnp.zeros(pad.shape, jnp.int32)
    pad[:, :n_words] = words_ref[...]
    per_row = half_c // 2 // 32
    for i0 in range(0, half_r, 8):
        for j0 in range(0, half_c, wide):
            i = iota((8, wide), 0) + i0
            j = iota((8, wide), 1) + j0
            which = jnp.right_shift(i, 1) * per_row + jnp.right_shift(j, 6)
            shift = jnp.bitwise_and(jnp.right_shift(j, 1), 31)
            for t in range(tiles):
                words = jnp.broadcast_to(pad[t : t + 1, :], (8, wide))
                word = jnp.take_along_axis(words, which, axis=1)
                bit = jnp.bitwise_and(jnp.right_shift(word, shift), 1)
                valid_ref[t * half_r + i0 : t * half_r + i0 + 8, j0 : j0 + wide] = bit.astype(jnp.float32)
    fetch.wait()
    for g in range(tiles // chunk):
        field = field_ref[g * fr : (g + 1) * fr, :]
        blurred = jnp.dot(rowd[...], field, preferred_element_type=jnp.float32).astype(jnp.bfloat16)
        pred_ref[g * fh : (g + 1) * fh, :] = jnp.dot(
            blurred, col[...], preferred_element_type=jnp.float32
        ).astype(jnp.bfloat16)


def after(sizes, n_tile, pick_ref, pred_ref, valid_ref, colt_ref, rowt_ref, own_ref, *refs):
    tiles, chunk, members, rows, cols = sizes
    half_r, half_c = rows // 2, cols // 2
    arrived, out_ref, scenes, update, sems = refs[:n_tile], refs[n_tile], *refs[n_tile + 1 :]
    fields = chunk * members
    fr, fh = fields * rows, fields * half_r
    for p, block in enumerate((*arrived, own_ref)):
        for r in range(CAP):
            for kind in range(2):
                scenes[p * CAP + r, kind] = block[kind, r]
    pr, ph = rowt_ref.shape
    cuts = fr // pr
    copies = []
    for g in range(tiles // chunk):
        parts = []
        for t in range(g * chunk, (g + 1) * chunk):
            seen = scenes[pick_ref[t], 0].astype(jnp.float32)
            sigma = scenes[pick_ref[t], 1].astype(jnp.float32)
            weight = valid_ref[t * half_r : (t + 1) * half_r, :] / (sigma * sigma)
            for m in range(members):
                at = (t * members + m) * half_r
                gap = seen - pred_ref[at : at + half_r, :].astype(jnp.float32)
                parts.append((gap * weight).astype(jnp.bfloat16))
        misfit = jnp.concatenate(parts, axis=0)
        spread = jnp.dot(misfit, colt_ref[...], preferred_element_type=jnp.float32).astype(jnp.bfloat16)
        for c in range(cuts):
            at = pl.ds(g * fr + c * pr, pr)
            update[at, :] = jnp.dot(
                rowt_ref[...], spread[c * ph : (c + 1) * ph, :], preferred_element_type=jnp.float32
            ).astype(jnp.bfloat16)
            copies.append(pltpu.make_async_copy(update.at[at, :], out_ref.at[at, :], sems.at[len(copies)]))
            copies[-1].start()
    for copy in copies:
        copy.wait()


def per_device(sim_lai, owner_ids, cloud_words, scene_lai, scene_sigma, mtf_taps):
    n_tile, n_mem = lax.axis_size("tile"), lax.axis_size("member")
    _, tiles, members, rows, cols = sim_lai.shape
    half_r, half_c = rows // 2, cols // 2
    chunk = chunk_tiles(tiles, members, rows)
    sizes = (tiles, chunk, members, rows, cols)
    fields = chunk * members
    fr, fh = fields * rows, fields * half_r
    cuts = PIECES if fields % PIECES == 0 else 1
    vmem = pl.BlockSpec(memory_space=pltpu.VMEM)
    smem = pl.BlockSpec(memory_space=pltpu.SMEM)
    here = lambda x: pltpu.with_memory_space_constraint(x, pltpu.VMEM)
    scalars = lambda x: pltpu.with_memory_space_constraint(x, pltpu.SMEM)
    steps = plan(n_tile, n_mem)
    block = pltpu.VMEM((2, CAP, half_r, half_c), jnp.bfloat16)
    *blocks, own, taps, words, owners = pl.pallas_call(
        lambda *refs: pack(steps, (n_tile, n_mem), *refs),
        out_shape=(
            *[block] * (n_tile + 1),
            pltpu.VMEM(mtf_taps.shape, jnp.float32),
            pltpu.VMEM(cloud_words.shape[1:], jnp.int32),
            pltpu.SMEM((tiles,), jnp.int32),
        ),
        in_specs=[smem] + [vmem] * 4,
        out_specs=[vmem] * (n_tile + 3) + [smem],
        name="pack",
    )(owner_ids, scene_lai[0, 0], scene_sigma[0, 0], mtf_taps, cloud_words[0])
    n_date = lax.axis_size("date")
    arrived = [here(lax.ppermute(blocks[p], GROUP, pairs(steps[p], n_date))) for p in range(n_tile)]
    pred, valid, colt, rowt, picks = pl.pallas_call(
        lambda *refs: before(sizes, (n_tile, n_mem), *refs),
        out_shape=(
            pltpu.VMEM((tiles * members * half_r, half_c), jnp.bfloat16),
            pltpu.VMEM((tiles * half_r, half_c), jnp.float32),
            pltpu.VMEM((half_c, cols), jnp.bfloat16),
            pltpu.VMEM((fr // cuts, fh // cuts), jnp.bfloat16),
            pltpu.SMEM((tiles,), jnp.int32),
        ),
        in_specs=[smem, vmem, vmem, pl.BlockSpec(memory_space=pl.ANY)],
        out_specs=[vmem] * 4 + [smem],
        scratch_shapes=[
            pltpu.VMEM((tiles, 128), jnp.int32),
            pltpu.VMEM((cols, half_c), jnp.bfloat16),
            pltpu.VMEM((fh, fr), jnp.bfloat16),
            pltpu.VMEM((tiles * members * rows, cols), jnp.bfloat16),
            pltpu.SemaphoreType.DMA,
        ],
        name="before",
    )(scalars(owners), here(taps), here(words), sim_lai.reshape(tiles * members * rows, cols))
    out = pl.pallas_call(
        lambda *refs: after(sizes, n_tile, *refs),
        out_shape=jax.ShapeDtypeStruct((tiles * members * rows, cols), jnp.bfloat16),
        in_specs=[smem] + [vmem] * (5 + n_tile),
        out_specs=pl.BlockSpec(memory_space=pl.ANY),
        scratch_shapes=[
            pltpu.VMEM(((n_tile + 1) * CAP, 2, half_r, half_c), jnp.bfloat16),
            pltpu.VMEM((tiles * members * rows, cols), jnp.bfloat16),
            pltpu.SemaphoreType.DMA((cuts * tiles // chunk,)),
        ],
        name="after",
    )(scalars(picks), *[here(x) for x in (pred, valid, colt, rowt, own)], *arrived)
    return out.reshape(sim_lai.shape)


def solution(mesh):
    placed = (
        P("date", ("region", "tile"), "member", None, None),
        P("date", ("region", "tile")),
        P("date", ("region", "tile"), None),
        P("date", ("region", "tile"), "member", None, None),
        P("date", ("region", "tile"), "member", None, None),
        P(),
    )
    return jax.shard_map(
        per_device,
        mesh=mesh,
        in_specs=placed,
        out_specs=P("date", ("region", "tile"), "member", None, None),
        check_vma=False,
    )
```
